512 devices in a mesh: tm: 16 (over x, z_hi, core), gy: 8 (over z_lo), gx: 4 (over y).
Axes of the slice: x: 4, y: 4, z: 16 (z_hi: 2, z_lo: 8; z = z_hi * 8 + z_lo), core: 2. Of those that a mesh axis runs over, the one named last changes fastest.
Arguments:
- initial_state: float32 [2, 32, 64, 128], P(None, 'gy', 'gx'), may hold values from 0 to 1
- slice_guess: float32 [16, 2, 32, 64, 128], P('tm', None, 'gy', 'gx'), may hold values from 0 to 1
- feed_rate: float32 [32, 64, 128], P('gy', 'gx'), may hold values from 0.02 to 0.2
- kill_rate: float32 [32, 64, 128], P('gy', 'gx'), may hold values from 0.03 to 0.12
Outputs:
- final_states: float32 [16, 2, 32, 64, 128], P('tm', None, 'gy', 'gx')
The draws below stay inside these ranges and needn't reach their ends.
All inputs are finite; a program needn't handle non-finite values.
Results may differ from the reference program's by a relative error of at most 0.0001.
Values sent between devices are 32-bit elements; how exact they have to be, the bound alone decides.
A program may use at most 64 MiB of HBM per device.

```python
import math
import jax
import jax.numpy as jnp

ITERS = 3
SLICES = 16
NX = 32
NY = 64
NZ = 128


def level_of(own_key, extent, shards, low, top_value):
    factor_of, own = 1.0, jax.random.fold_in(own_key, 6)
    for axis_at, blocks in shards:
        steps = jnp.exp(jax.random.uniform(jax.random.fold_in(own, axis_at), (blocks,), jnp.float32, low / len(shards), top_value / len(shards)))
        factor_of = factor_of * jnp.repeat(steps, extent[axis_at] // blocks).reshape([-1 if axis == axis_at else 1 for axis in range(len(extent))])
    return factor_of


def setup_inputs(seed: int = 0) -> dict:
    seeds = jax.random.split(jax.random.key(seed), 5)
    initial_state = jnp.clip(1.0 * jax.random.uniform(seeds[0], (2, NX, NY, NZ), jnp.float32) ** level_of(seeds[0], (2, NX, NY, NZ), ((1, 8), (2, 4)), -0.2, 0.2), 0.0, 1.0)
    slice_guess = jnp.clip(1.0 * jax.random.uniform(seeds[1], (SLICES, 2, NX, NY, NZ), jnp.float32) ** level_of(seeds[1], (SLICES, 2, NX, NY, NZ), ((0, 16), (2, 8), (3, 4)), -0.2, 0.2), 0.0, 1.0)
    feed_rate = jnp.clip(jnp.exp(math.log(0.2) - 2.3025851 * jax.random.uniform(seeds[2], (NX, NY, NZ), jnp.float32) ** level_of(seeds[2], (NX, NY, NZ), ((0, 8), (1, 4)), -0.2, 0.2)), 0.02, 0.2)
    kill_rate = jnp.clip(jnp.exp(math.log(0.12) - 1.3862944 * jax.random.uniform(seeds[3], (NX, NY, NZ), jnp.float32) ** level_of(seeds[3], (NX, NY, NZ), ((0, 8), (1, 4)), -0.2, 0.2)), 0.03, 0.12)
    return dict(initial_state=initial_state, slice_guess=slice_guess, feed_rate=feed_rate, kill_rate=kill_rate)


DIFF_U = 0.2
DIFF_V = 0.1
HALF_STEP = 0.5
WEIGHTS = ((5.0 / 24.0, 8.0 / 24.0, -1.0 / 24.0), (-1.0 / 24.0, 8.0 / 24.0, 5.0 / 24.0))


def restrict(grid_field):
    leading = grid_field.shape[:-3]
    size_x, size_y, size_z = grid_field.shape[-3:]
    blocks = grid_field.reshape(leading + (size_x // 2, 2, size_y // 2, 2, size_z // 2, 2))
    return 0.125 * jnp.sum(blocks, axis=(-5, -3, -1))


def prolong(grid_field):
    return jnp.repeat(jnp.repeat(jnp.repeat(grid_field, 2, axis=-3), 2, axis=-2), 2, axis=-1)


def source_terms(laplacian, state, feed_rate, kill_rate):
    conc_u = state[..., 0, :, :, :]
    conc_v = state[..., 1, :, :, :]
    reaction = conc_u * conc_v * conc_v
    rate_u = DIFF_U * laplacian[..., 0, :, :, :] - reaction + feed_rate * (1.0 - conc_u)
    rate_v = DIFF_V * laplacian[..., 1, :, :, :] + reaction - (feed_rate + kill_rate) * conc_v
    return jnp.stack([rate_u, rate_v], axis=-4)


def reaction_rates(state, feed_rate, kill_rate, spacing):
    summed = -6.0 * state
    for axis_index in (-3, -2, -1):
        summed = summed + jnp.roll(state, 1, axis_index) + jnp.roll(state, -1, axis_index)
    return source_terms(summed / (spacing * spacing), state, feed_rate, kill_rate)


def quadrature(values, interval):
    return WEIGHTS[interval][0] * values[0] + WEIGHTS[interval][1] * values[1] + WEIGHTS[interval][2] * values[2]


def reference(initial_state, slice_guess, feed_rate, kill_rate):
    coarse_feed = restrict(feed_rate)
    coarse_kill = restrict(kill_rate)
    guess_rates = jnp.zeros_like(slice_guess)
    node_values = [slice_guess, slice_guess, slice_guess]
    values = [guess_rates, guess_rates, guess_rates]
    coarse_end = restrict(slice_guess)
    coarse_anchor = restrict(initial_state)
    for sweep_index in range(ITERS):
        integral_zero = quadrature(values, 0)
        integral_one = quadrature(values, 1)
        start_state = jnp.concatenate([initial_state[None], node_values[2][:-1]], axis=0)
        coarse_start = jnp.concatenate([coarse_anchor[None], coarse_end[:-1]], axis=0)
        rate_zero = reaction_rates(start_state, feed_rate, kill_rate, 1.0)
        node_one = start_state + HALF_STEP * (rate_zero - values[0]) + integral_zero
        rate_one = reaction_rates(node_one, feed_rate, kill_rate, 1.0)
        node_two = node_one + HALF_STEP * (rate_one - values[1]) + integral_one
        rate_two = reaction_rates(node_two, feed_rate, kill_rate, 1.0)
        fresh = [rate_zero, rate_one, rate_two]
        fine_zero = quadrature(fresh, 0)
        fine_one = quadrature(fresh, 1)
        rest_zero = restrict(start_state)
        rest_one = restrict(node_one)
        rest_two = restrict(node_two)
        coarse_rate_zero = reaction_rates(rest_zero, coarse_feed, coarse_kill, 2.0)
        coarse_rate_one = reaction_rates(rest_one, coarse_feed, coarse_kill, 2.0)
        coarse_one = coarse_start + HALF_STEP * (reaction_rates(coarse_start, coarse_feed, coarse_kill, 2.0) - coarse_rate_zero) + restrict(fine_zero)
        coarse_two = coarse_one + HALF_STEP * (reaction_rates(coarse_one, coarse_feed, coarse_kill, 2.0) - coarse_rate_one) + restrict(fine_one)
        node_one = node_one + prolong(coarse_one - rest_one)
        node_two = node_two + prolong(coarse_two - rest_two)
        if sweep_index + 1 < ITERS:
            values = [rate_zero, reaction_rates(node_one, feed_rate, kill_rate, 1.0), reaction_rates(node_two, feed_rate, kill_rate, 1.0)]
        node_values = [start_state, node_one, node_two]
        coarse_end = coarse_two
    return node_values[2]
```

```python
import functools

import jax
import jax.numpy as jnp
from jax import lax
from jax.experimental import pallas as pl
from jax.experimental.pallas import tpu as pltpu
from jax.sharding import PartitionSpec as P

ITERS = 3
DIFF = (0.2, 0.1)
HALF_STEP = 0.5
WEIGHTS = ((5.0 / 24.0, 8.0 / 24.0, -1.0 / 24.0), (-1.0 / 24.0, 8.0 / 24.0, 5.0 / 24.0))

PLANES, ROWS, LANES = 4, 16, 128
TALL, LOW, WINDOW, OWN = 40, 8, 24, 12
HALO = 3
N_SEMS = 112


def kernel(dims, init_ref, guess_ref, feed_ref, kill_ref, out_ref,
           s_buf, c_buf, u_buf, w_buf, v1_buf, v2_buf, fk_buf, g0_buf, a0_buf, a1_buf, q_buf, o_buf,
           send_sem, recv_sem):
    nt, ng, nx = dims
    chips = ng // 2
    blocks = nt // ng
    n, g, y = lax.axis_index("tm"), lax.axis_index("gy"), lax.axis_index("gx")

    def home_of(slice_at, tile):
        return slice_at, tile

    def role_of(slice_at, tile):
        return 2 * blocks * (tile // 2) + 2 * (slice_at // ng) + tile % 2, slice_at % ng

    def device(place, column):
        return {"tm": place[0], "gy": place[1], "gx": column}

    def is_me(place):
        return jnp.logical_and(place[0] == n, place[1] == g)

    across, block, core = n // (2 * blocks), (n // 2) % blocks, n % 2
    t = 2 * across + core
    m = ng * block + g

    s_to = role_of((n + 1) % nt, g)
    s_from = home_of((m + nt - 1) % nt, t)
    fk_to = role_of((g + nt - ng // 2 + ng * block + 2 * ((across + chips - g // 2) % chips) + core) % nt, g)
    fk_at = (m - t + ng // 2 + nt) % nt
    fk_from = (2 * blocks * ((t // 2 + (fk_at % ng) // 2) % chips) + 2 * (fk_at // ng) + fk_at % 2, t)
    out_to = home_of(m, t)
    out_from = role_of(n, g)
    later, earlier = role_of((m + 1) % nt, t), role_of((m + nt - 1) % nt, t)
    sides = [(dx, dy) for dx in (-1, 0, 1) for dy in (-1, 0, 1) if (dx, dy) != (0, 0)]
    faces = [(dx, dy) for dx, dy in sides if dx == 0 or dy == 0]

    def neighbour(dx, dy):
        return device(role_of(m, (t + dx + ng) % ng), (y + dy + nx) % nx)

    barrier = pltpu.get_barrier_semaphore()
    partners = [device(place, y) for place in (s_from, fk_from, out_from, earlier, later)]
    partners += [neighbour(dx, dy) for dx, dy in sides]
    for partner in partners:
        pl.semaphore_signal(barrier, inc=1, device_id=partner, device_id_type=pl.DeviceIdType.MESH)
    pl.semaphore_wait(barrier, len(partners))

    used = [0]
    started = []

    def remote(src, dst, where):
        index = used[0]
        used[0] += 1
        return pltpu.make_async_remote_copy(
            src_ref=src, dst_ref=dst, send_sem=send_sem.at[index], recv_sem=recv_sem.at[index],
            device_id=where, device_id_type=pl.DeviceIdType.MESH), index

    def move(src, dst, place, column, when=None):
        copy, index = remote(src, dst, device(place, column))
        local = pltpu.make_async_copy(src, dst, recv_sem.at[index])
        away = jnp.logical_not(is_me(place))
        if when is not None:
            here = jnp.logical_and(when, is_me(place))
            away = jnp.logical_and(when, away)
        else:
            here = is_me(place)

        @pl.when(away)
        def _():
            copy.start()

        @pl.when(here)
        def _():
            local.start()

        started.append((copy, away))
        return copy

    def halo_piece(dx, dy, lead, width, own_x, count, width_x):
        if dx == 0:
            sx, tx = pl.ds(own_x, count), pl.ds(own_x, count)
        elif dx > 0:
            sx, tx = pl.ds(own_x + count - width_x, width_x), pl.ds(own_x - width_x, width_x)
        else:
            sx, tx = pl.ds(own_x, width_x), pl.ds(own_x + count, width_x)
        if dy == 0:
            sy, ty = pl.ds(OWN, ROWS), pl.ds(OWN, ROWS)
        elif dy > 0:
            sy, ty = pl.ds(OWN + ROWS - width, width), pl.ds(OWN - width, width)
        else:
            sy, ty = pl.ds(OWN, width), pl.ds(OWN + ROWS, width)
        return (lead, sx, sy), (lead, tx, ty)

    def exchange(buf, fields, where, width, own_x, count, width_x):
        copies = []
        for dx, dy in where:
            src, dst = halo_piece(dx, dy, pl.ds(0, fields), width, own_x, count, width_x)
            copy, _ = remote(buf.at[src], buf.at[dst], neighbour(dx, dy))
            copy.start()
            started.append((copy, None))
            copies.append(copy)
        return copies

    def arrive(copies):
        for copy in copies:
            copy.wait_recv()

    own = (pl.ds(0, 2), pl.ds(HALO, PLANES), pl.ds(OWN, ROWS))
    own_c = (pl.ds(0, 2), pl.ds(1, 2), pl.ds(OWN, ROWS))

    fk_own = (pl.ds(2, PLANES), pl.ds(OWN, ROWS))
    feed_in = move(feed_ref, fk_buf.at[(0, *fk_own)], fk_to, y)
    kill_in = move(kill_ref, fk_buf.at[(1, *fk_own)], fk_to, y)
    first_s = s_buf.at[0]
    last_home = n == nt - 1
    mark = used[0]
    s_in = move(guess_ref.at[0], first_s.at[own], s_to, y, jnp.logical_not(last_home))
    used[0] = mark
    move(init_ref, first_s.at[own], s_to, y, last_home)

    row = lax.broadcasted_iota(jnp.int32, (WINDOW, LANES), 0)
    lane = lax.broadcasted_iota(jnp.int32, (WINDOW, LANES), 1)
    even_row, even_lane = row % 2 == 0, lane % 2 == 0

    def rows(by=0):
        return pl.ds(LOW + by, WINDOW)

    def turn(value, by, axis):
        size = value.shape[axis]
        return pltpu.roll(value, by % size, axis % value.ndim)

    def source(lap_u, lap_v, u, v, feed, both):
        reaction = u * v * v
        return lap_u - reaction + feed * (1.0 - u), lap_v + reaction - both * v

    def fine_rates(buf, first, at, feed_at, count):
        laps, mids = [], []
        for field in range(2):
            f = first + field
            mid = buf[f, pl.ds(at, count), rows(), :]
            total = buf[f, pl.ds(at - 1, count), rows(), :] + buf[f, pl.ds(at + 1, count), rows(), :]
            total = total + buf[f, pl.ds(at, count), rows(-1), :] + buf[f, pl.ds(at, count), rows(1), :]
            total = total + turn(mid, 1, -1) + turn(mid, -1, -1)
            laps.append(DIFF[field] * (total - 6.0 * mid))
            mids.append(mid)
        feed = fk_buf[0, pl.ds(feed_at, count), rows(), :]
        both = fk_buf[2, pl.ds(feed_at, count), rows(), :]
        return mids, source(laps[0], laps[1], mids[0], mids[1], feed, both)

    def pair_sum(value):
        value = value + jnp.where(even_row, turn(value, -1, -2), turn(value, 1, -2))
        return value + jnp.where(even_lane, turn(value, -1, -1), turn(value, 1, -1))

    def restrict(first, second):
        return 0.125 * pair_sum(first + second)

    def coarse_rates(below, mid, above, feed, both):
        laps = []
        for field in range(2):
            total = below[field] + above[field] + turn(mid[field], 2, -2) + turn(mid[field], -2, -2)
            total = total + turn(mid[field], 2, -1) + turn(mid[field], -2, -1)
            laps.append((0.25 * DIFF[field]) * (total - 6.0 * mid[field]))
        return source(laps[0], laps[1], mid[0], mid[1], feed, both)

    arrive((feed_in, kill_in))
    fk_halo = exchange(fk_buf, 2, sides, 2, 2, PLANES, 2)
    arrive((s_in,))
    s_halo = exchange(first_s, 2, sides, HALO, HALO, PLANES, HALO)
    c_halo = []
    arrive(fk_halo)
    for p in range(8):
        fk_buf[2, p, rows(), :] = fk_buf[0, p, rows(), :] + fk_buf[1, p, rows(), :]
    coarse_feed = [restrict(fk_buf[0, 2 + 2 * p, rows(), :], fk_buf[0, 3 + 2 * p, rows(), :]) for p in range(2)]
    coarse_kill = [restrict(fk_buf[1, 2 + 2 * p, rows(), :], fk_buf[1, 3 + 2 * p, rows(), :]) for p in range(2)]
    coarse_both = [coarse_feed[p] + coarse_kill[p] for p in range(2)]

    for k in range(ITERS):
        s_now, c_now, w_now = s_buf.at[k], c_buf.at[k], w_buf.at[k]
        last = k == ITERS - 1
        if k > 0:
            u_old = u_buf.at[k - 1]
            arrive(u_halo)
            for p in range(0, 8, 2):
                _, one = fine_rates(u_old, 0, p + 1, p, 2)
                _, two = fine_rates(u_old, 2, p + 1, p, 2)
                for field in range(2):
                    zero = g0_buf[field, pl.ds(p, 2), rows(), :]
                    a0_buf[field, pl.ds(p, 2), rows(), :] = (
                        (WEIGHTS[0][0] - HALF_STEP) * zero + WEIGHTS[0][1] * one[field] + WEIGHTS[0][2] * two[field])
                    a1_buf[field, pl.ds(p, 2), rows(), :] = (
                        WEIGHTS[1][0] * zero + (WEIGHTS[1][1] - HALF_STEP) * one[field] + WEIGHTS[1][2] * two[field])
        arrive(s_halo)
        for p in range(0, 8, 2):
            mids, rates = fine_rates(s_now, 0, p + 1, p, 2)
            for field in range(2):
                node = mids[field] + HALF_STEP * rates[field]
                if k > 0:
                    node = node + a0_buf[field, pl.ds(p, 2), rows(), :]
                g0_buf[field, pl.ds(p, 2), rows(), :] = rates[field]
                v1_buf[field, pl.ds(p, 2), rows(), :] = node
        for p in range(0, 6, 2):
            mids, rates = fine_rates(v1_buf, 0, p + 1, p + 1, 2)
            for field in range(2):
                node = mids[field] + HALF_STEP * rates[field]
                if k > 0:
                    node = node + a1_buf[field, pl.ds(p + 1, 2), rows(), :]
                v2_buf[field, pl.ds(p, 2), rows(), :] = node
                q_buf[field, pl.ds(p, 2), rows(), :] = rates[field]
        rest_s = [[restrict(s_now[f, 1 + 2 * p, rows(), :], s_now[f, 2 + 2 * p, rows(), :]) for f in range(2)]
                  for p in range(4)]
        if k == 0:
            coarse = rest_s
            for p in range(2):
                for f in range(2):
                    c_now[f, 1 + p, rows(), :] = coarse[1 + p][f]
        else:
            arrive(c_halo)
            coarse = [[c_now[f, p, rows(), :] for f in range(2)] for p in range(4)]
        rest_v1 = [[restrict(v1_buf[f, 2 * p, rows(), :], v1_buf[f, 1 + 2 * p, rows(), :]) for f in range(2)]
                   for p in range(4)]
        integral = []
        w_one = []
        for p in range(2):
            _, two = fine_rates(v2_buf, 0, 2 * p + 1, 2 * p + 2, 2)
            sums = []
            for f in range(2):
                zero = g0_buf[f, pl.ds(2 + 2 * p, 2), rows(), :]
                one = q_buf[f, pl.ds(1 + 2 * p, 2), rows(), :]
                whole = [weight[0] * zero + weight[1] * one + weight[2] * two[f] for weight in WEIGHTS]
                sums.append([restrict(q[0], q[1]) for q in whole])
            integral.append(sums)
            rate_c = coarse_rates(coarse[p], coarse[p + 1], coarse[p + 2], coarse_feed[p], coarse_both[p])
            rate_s = coarse_rates(rest_s[p], rest_s[p + 1], rest_s[p + 2], coarse_feed[p], coarse_both[p])
            w_one.append([coarse[p + 1][f] + HALF_STEP * (rate_c[f] - rate_s[f]) + sums[f][0] for f in range(2)])
            for f in range(2):
                w_now[f, 1 + p, pl.ds(OWN, ROWS), :] = w_one[p][f][OWN - LOW : OWN - LOW + ROWS]
        w_halo = exchange(w_now, 2, faces, 2, 1, 2, 1)
        rest_v2 = [[restrict(v2_buf[f, 1 + 2 * p, rows(), :], v2_buf[f, 2 + 2 * p, rows(), :]) for f in range(2)]
                   for p in range(2)]
        rate_v1 = [coarse_rates(rest_v1[p], rest_v1[p + 1], rest_v1[p + 2], coarse_feed[p], coarse_both[p])
                   for p in range(2)]
        arrive(w_halo)
        coarse_w = [[w_now[f, p, rows(), :] for f in range(2)] for p in range(4)]
        for p in range(2):
            rate_w = coarse_rates(coarse_w[p], coarse_w[p + 1], coarse_w[p + 2], coarse_feed[p], coarse_both[p])
            for f in range(2):
                w_two = w_one[p][f] + HALF_STEP * (rate_w[f] - rate_v1[p][f]) + integral[p][f][1]
                up_one = w_one[p][f] - rest_v1[p + 1][f]
                up_two = w_two - rest_v2[p][f]
                keep = slice(OWN - LOW, OWN - LOW + ROWS)
                for q in range(2):
                    at = 2 * p + q
                    two = v2_buf[f, at + 1, rows(), :] + up_two
                    if last:
                        o_buf[f, at, :, :] = two[keep]
                    else:
                        one = v1_buf[f, at + 2, rows(), :] + up_one
                        u_buf[k, f, HALO + at, pl.ds(OWN, ROWS), :] = one[keep]
                        u_buf[k, 2 + f, HALO + at, pl.ds(OWN, ROWS), :] = two[keep]
                if not last:
                    w_buf[ITERS + k, f, 1 + p, pl.ds(OWN, ROWS), :] = w_two[keep]
        if not last:
            u_now, s_next, c_next = u_buf.at[k], s_buf.at[k + 1], c_buf.at[k + 1]
            shifted = []
            for src, dst, kept in (
                (u_now.at[(pl.ds(2, 2), *own[1:])], s_next.at[own], s_now.at[own]),
                (w_buf.at[(ITERS + k, *own_c)], c_next.at[own_c], c_now.at[own_c]),
            ):
                copy, index = remote(src, dst, device(later, y))
                stay = pltpu.make_async_copy(kept, dst, recv_sem.at[index])
                onward = m < nt - 1

                @pl.when(onward)
                def _(copy=copy):
                    copy.start()

                @pl.when(m == 0)
                def _(stay=stay):
                    stay.start()

                started.append((copy, onward))
                shifted.append(copy)
            u_halo = exchange(u_now, 4, sides, HALO, HALO, PLANES, HALO)
            arrive(shifted[:1])
            s_halo = exchange(s_next, 2, sides, HALO, HALO, PLANES, HALO)
            arrive(shifted[1:])
            c_halo = exchange(c_next, 2, faces, 2, 1, 2, 1)

    out_in = move(o_buf, out_ref.at[0], out_to, y)
    arrive((out_in,))
    for copy, when in started:
        if when is None:
            copy.wait_send()
        else:

            @pl.when(when)
            def _(copy=copy):
                copy.wait_send()

    assert used[0] <= N_SEMS


def solution(mesh):
    dims = (mesh.shape["tm"], mesh.shape["gy"], mesh.shape["gx"])

    def shards(initial_state, slice_guess, feed_rate, kill_rate):
        buffers = [
            (ITERS, 2, 10, TALL, LANES),
            (ITERS, 2, 4, TALL, LANES),
            (ITERS - 1, 4, 10, TALL, LANES),
            (2 * ITERS - 1, 2, 4, TALL, LANES),
            (2, 8, TALL, LANES),
            (2, 6, TALL, LANES),
            (3, 8, TALL, LANES),
            (2, 8, TALL, LANES),
            (2, 8, TALL, LANES),
            (2, 8, TALL, LANES),
            (2, 6, TALL, LANES),
            (2, PLANES, ROWS, LANES),
        ]
        return pl.pallas_call(
            functools.partial(kernel, dims),
            out_shape=jax.ShapeDtypeStruct((1, 2, PLANES, ROWS, LANES), jnp.float32),
            in_specs=[pl.BlockSpec(memory_space=pl.ANY)] * 4,
            out_specs=pl.BlockSpec(memory_space=pl.ANY),
            scratch_shapes=[pltpu.VMEM(shape, jnp.float32) for shape in buffers]
            + [pltpu.SemaphoreType.DMA((N_SEMS,)), pltpu.SemaphoreType.DMA((N_SEMS,))],
            compiler_params=pltpu.CompilerParams(collective_id=0, has_side_effects=True),
        )(initial_state, slice_guess, feed_rate, kill_rate)

    in_specs = (
        P(None, "gy", "gx", None),
        P("tm", None, "gy", "gx", None),
        P("gy", "gx", None),
        P("gy", "gx", None),
    )
    out_specs = P("tm", None, "gy", "gx", None)
    return jax.shard_map(shards, mesh=mesh, in_specs=in_specs, out_specs=out_specs, check_vma=False)
```

```python
import functools

import jax
import jax.numpy as jnp
from jax import lax
from jax.experimental import pallas as pl
from jax.experimental.pallas import tpu as pltpu
from jax.sharding import PartitionSpec as P

ITERS = 3
DIFF = (0.2, 0.1)
HALF_STEP = 0.5
WEIGHTS = ((5.0 / 24.0, 8.0 / 24.0, -1.0 / 24.0), (-1.0 / 24.0, 8.0 / 24.0, 5.0 / 24.0))

PLANES, ROWS, LANES = 4, 16, 128
TALL, LOW, WINDOW, OWN = 40, 8, 24, 12
HALO = 5
SHIFT = 2
N_SEMS = 128


def kernel(dims, init_ref, guess_ref, feed_ref, kill_ref, out_ref,
           s_buf, c_buf, u_buf, w_buf, v1_buf, v2_buf, fk_buf, g0_buf, g1_buf, a0_buf, a1_buf, o_buf,
           send_sem, recv_sem):
    nt, ng, nx = dims
    chips = ng // 2
    blocks = nt // ng
    n, g, y = lax.axis_index("tm"), lax.axis_index("gy"), lax.axis_index("gx")

    def home_of(slice_at, tile):
        return slice_at, tile

    def role_of(slice_at, tile):
        along = (slice_at + SHIFT) % nt
        turned = (tile + 2 * (slice_at // (2 * blocks))) % ng
        return 2 * blocks * (turned // 2) + 2 * (along // ng) + turned % 2, along % ng

    def device(place, column):
        return {"tm": place[0], "gy": place[1], "gx": column}

    def is_me(place):
        return jnp.logical_and(place[0] == n, place[1] == g)

    across, block, core = n // (2 * blocks), (n // 2) % blocks, n % 2
    along = ng * block + g
    m = (along + nt - SHIFT) % nt
    t = (2 * across + core + ng - 2 * (m // (2 * blocks))) % ng

    s_to = role_of((n + 1) % nt, g)
    s_from = home_of((m + nt - 1) % nt, t)
    fk_along = g + nt - ng // 2 + ng * block + 2 * ((across + chips - g // 2) % chips) + core
    fk_to = role_of((fk_along + nt - SHIFT) % nt, g)
    fk_at = (along - t + ng // 2 + nt) % nt
    fk_from = (2 * blocks * ((t // 2 + (fk_at % ng) // 2) % chips) + 2 * (fk_at // ng) + fk_at % 2, t)
    out_to = home_of(m, t)
    out_from = role_of(n, g)
    later, earlier = role_of((m + 1) % nt, t), role_of((m + nt - 1) % nt, t)
    near = [(dx, dy) for dx in (-1, 0, 1) for dy in (-1, 0, 1) if (dx, dy) != (0, 0)]
    wide = near + [(dx, dy) for dx in (-2, 2) for dy in (-1, 0, 1)]

    def neighbour(dx, dy):
        return device(role_of(m, (t + dx + ng) % ng), (y + dy + nx) % nx)

    barrier = pltpu.get_barrier_semaphore()
    partners = [device(place, y) for place in (s_from, fk_from, out_from, earlier, later)]
    partners += [neighbour(dx, dy) for dx, dy in wide]
    for partner in partners:
        pl.semaphore_signal(barrier, inc=1, device_id=partner, device_id_type=pl.DeviceIdType.MESH)
    pl.semaphore_wait(barrier, len(partners))

    used = [0]
    started = []

    def remote(src, dst, where):
        index = used[0]
        used[0] += 1
        return pltpu.make_async_remote_copy(
            src_ref=src, dst_ref=dst, send_sem=send_sem.at[index], recv_sem=recv_sem.at[index],
            device_id=where, device_id_type=pl.DeviceIdType.MESH), index

    def move(src, dst, place, column, when=None):
        copy, index = remote(src, dst, device(place, column))
        local = pltpu.make_async_copy(src, dst, recv_sem.at[index])
        away = jnp.logical_not(is_me(place))
        if when is not None:
            here = jnp.logical_and(when, is_me(place))
            away = jnp.logical_and(when, away)
        else:
            here = is_me(place)

        @pl.when(away)
        def _():
            copy.start()

        @pl.when(here)
        def _():
            local.start()

        started.append((copy, away))
        return copy

    def exchange(buf, fields, where, own_x, count, width_x, width_y):
        copies = []
        for dx, dy in where:
            planes = count if dx == 0 else min(count, width_x - count * (abs(dx) - 1))
            from_x = own_x + count - planes if dx > 0 else own_x
            to_x = from_x - dx * count
            rows_sent = ROWS if dy == 0 else width_y
            from_y = OWN + ROWS - rows_sent if dy > 0 else OWN
            to_y = from_y - dy * ROWS
            src = buf.at[pl.ds(0, fields), pl.ds(from_x, planes), pl.ds(from_y, rows_sent)]
            dst = buf.at[pl.ds(0, fields), pl.ds(to_x, planes), pl.ds(to_y, rows_sent)]
            copy, _ = remote(src, dst, neighbour(dx, dy))
            copy.start()
            started.append((copy, None))
            copies.append(copy)
        return copies

    def arrive(copies):
        for copy in copies:
            copy.wait_recv()

    own = (pl.ds(0, 2), pl.ds(HALO, PLANES), pl.ds(OWN, ROWS))
    own_c = (pl.ds(0, 2), pl.ds(2, 2), pl.ds(OWN, ROWS))

    fk_own = (pl.ds(4, PLANES), pl.ds(OWN, ROWS))
    first_s = s_buf.at[0]
    last_home = n == nt - 1
    mark = used[0]
    s_in = move(guess_ref.at[0], first_s.at[own], s_to, y, jnp.logical_not(last_home))
    used[0] = mark
    move(init_ref, first_s.at[own], s_to, y, last_home)
    feed_in = move(feed_ref, fk_buf.at[(0, *fk_own)], fk_to, y)
    kill_in = move(kill_ref, fk_buf.at[(1, *fk_own)], fk_to, y)

    row = lax.broadcasted_iota(jnp.int32, (WINDOW, LANES), 0)
    lane = lax.broadcasted_iota(jnp.int32, (WINDOW, LANES), 1)
    even_row, even_lane = row % 2 == 0, lane % 2 == 0

    def rows(by=0):
        return pl.ds(LOW + by, WINDOW)

    def turn(value, by, axis):
        size = value.shape[axis]
        return pltpu.roll(value, by % size, axis % value.ndim)

    def source(lap_u, lap_v, u, v, feed, both):
        reaction = u * v * v
        return lap_u - reaction + feed * (1.0 - u), lap_v + reaction - both * v

    def fine_rates(buf, first, at, feed_at, count):
        laps, mids = [], []
        for field in range(2):
            f = first + field
            mid = buf[f, pl.ds(at, count), rows(), :]
            total = buf[f, pl.ds(at - 1, count), rows(), :] + buf[f, pl.ds(at + 1, count), rows(), :]
            total = total + buf[f, pl.ds(at, count), rows(-1), :] + buf[f, pl.ds(at, count), rows(1), :]
            total = total + turn(mid, 1, -1) + turn(mid, -1, -1)
            laps.append(DIFF[field] * (total - 6.0 * mid))
            mids.append(mid)
        feed = fk_buf[0, pl.ds(feed_at, count), rows(), :]
        both = fk_buf[2, pl.ds(feed_at, count), rows(), :]
        return mids, source(laps[0], laps[1], mids[0], mids[1], feed, both)

    def pair_sum(value):
        value = value + jnp.where(even_row, turn(value, -1, -2), turn(value, 1, -2))
        return value + jnp.where(even_lane, turn(value, -1, -1), turn(value, 1, -1))

    def restrict(first, second):
        return 0.125 * pair_sum(first + second)

    def coarse_rates(below, mid, above, feed, both):
        laps = []
        for field in range(2):
            total = below[field] + above[field] + turn(mid[field], 2, -2) + turn(mid[field], -2, -2)
            total = total + turn(mid[field], 2, -1) + turn(mid[field], -2, -1)
            laps.append((0.25 * DIFF[field]) * (total - 6.0 * mid[field]))
        return source(laps[0], laps[1], mid[0], mid[1], feed, both)

    def send_states(buf):
        return exchange(buf, buf.shape[0], wide, HALO, PLANES, HALO, HALO)

    arrive((s_in,))
    s_halo = send_states(first_s)
    c_halo = []
    arrive((feed_in, kill_in))
    fk_halo = exchange(fk_buf, 2, near, 4, PLANES, 4, 4)
    arrive(fk_halo)
    for p in range(0, 12, 2):
        both = fk_buf[0, pl.ds(p, 2), rows(), :] + fk_buf[1, pl.ds(p, 2), rows(), :]
        fk_buf[2, pl.ds(p, 2), rows(), :] = both
    coarse_feed, coarse_both = [], []
    for p in range(4):
        feed, kill = [restrict(fk_buf[f, 2 + 2 * p, rows(), :], fk_buf[f, 3 + 2 * p, rows(), :]) for f in range(2)]
        coarse_feed.append(feed)
        coarse_both.append(feed + kill)

    for k in range(ITERS):
        s_now, c_now = s_buf.at[k], c_buf.at[k]
        last = k == ITERS - 1
        if k > 0:
            u_old = u_buf.at[k - 1]
            arrive(u_halo)
            for p in range(0, 12, 2):
                _, one = fine_rates(u_old, 0, p + 1, p, 2)
                _, two = fine_rates(u_old, 2, p + 1, p, 2)
                for field in range(2):
                    zero = g0_buf[field, pl.ds(p, 2), rows(), :]
                    a0_buf[field, pl.ds(p, 2), rows(), :] = (
                        (WEIGHTS[0][0] - HALF_STEP) * zero + WEIGHTS[0][1] * one[field] + WEIGHTS[0][2] * two[field])
                    a1_buf[field, pl.ds(p, 2), rows(), :] = (
                        WEIGHTS[1][0] * zero + (WEIGHTS[1][1] - HALF_STEP) * one[field] + WEIGHTS[1][2] * two[field])
        arrive(s_halo)
        for p in range(0, 12, 2):
            mids, rates = fine_rates(s_now, 0, p + 1, p, 2)
            for field in range(2):
                node = mids[field] + HALF_STEP * rates[field]
                if k > 0:
                    node = node + a0_buf[field, pl.ds(p, 2), rows(), :]
                g0_buf[field, pl.ds(p, 2), rows(), :] = rates[field]
                v1_buf[field, pl.ds(p, 2), rows(), :] = node
        for p in range(0, 10, 2):
            mids, rates = fine_rates(v1_buf, 0, p + 1, p + 1, 2)
            for field in range(2):
                node = mids[field] + HALF_STEP * rates[field]
                if k > 0:
                    node = node + a1_buf[field, pl.ds(p + 1, 2), rows(), :]
                v2_buf[field, pl.ds(p, 2), rows(), :] = node
                g1_buf[field, pl.ds(p, 2), rows(), :] = rates[field]
        rest_s = [[restrict(s_now[f, 1 + 2 * p, rows(), :], s_now[f, 2 + 2 * p, rows(), :]) for f in range(2)]
                  for p in range(6)]
        if k == 0:
            coarse = rest_s
            for p in range(2, 4):
                for f in range(2):
                    c_now[f, p, rows(), :] = coarse[p][f]
        else:
            arrive(c_halo)
            coarse = [[c_now[f, p, rows(), :] for f in range(2)] for p in range(6)]
        w_one, late = [], []
        for p in range(4):
            _, two = fine_rates(v2_buf, 0, 2 * p + 1, 2 * p + 2, 2)
            rate_c = coarse_rates(coarse[p], coarse[p + 1], coarse[p + 2], coarse_feed[p], coarse_both[p])
            rate_s = coarse_rates(rest_s[p], rest_s[p + 1], rest_s[p + 2], coarse_feed[p], coarse_both[p])
            values, later_sums = [], []
            for f in range(2):
                zero = g0_buf[f, pl.ds(2 + 2 * p, 2), rows(), :]
                one = g1_buf[f, pl.ds(1 + 2 * p, 2), rows(), :]
                first, second = [w[0] * zero + w[1] * one + w[2] * two[f] for w in WEIGHTS]
                values.append(coarse[p + 1][f] + HALF_STEP * (rate_c[f] - rate_s[f]) + restrict(first[0], first[1]))
                later_sums.append(restrict(second[0], second[1]) if p in (1, 2) else None)
            w_one.append(values)
            late.append(later_sums)
        rest_v1 = [[restrict(v1_buf[f, 2 + 2 * p, rows(), :], v1_buf[f, 3 + 2 * p, rows(), :]) for f in range(2)]
                   for p in range(4)]
        keep = slice(OWN - LOW, OWN - LOW + ROWS)
        for p in (1, 2):
            rate_w = coarse_rates(w_one[p - 1], w_one[p], w_one[p + 1], coarse_feed[p], coarse_both[p])
            rate_v1 = coarse_rates(rest_v1[p - 1], rest_v1[p], rest_v1[p + 1], coarse_feed[p], coarse_both[p])
            for f in range(2):
                w_two = w_one[p][f] + HALF_STEP * (rate_w[f] - rate_v1[f]) + late[p][f]
                rest_v2 = restrict(v2_buf[f, 1 + 2 * p, rows(), :], v2_buf[f, 2 + 2 * p, rows(), :])
                for at in (2 * p - 2, 2 * p - 1):
                    two = v2_buf[f, 3 + at, rows(), :] + (w_two - rest_v2)
                    if last:
                        o_buf[f, at, :, :] = two[keep]
                    else:
                        one = v1_buf[f, 4 + at, rows(), :] + (w_one[p][f] - rest_v1[p][f])
                        u_buf[k, f, HALO + at, pl.ds(OWN, ROWS), :] = one[keep]
                        u_buf[k, 2 + f, HALO + at, pl.ds(OWN, ROWS), :] = two[keep]
                if not last:
                    w_buf[k, f, p - 1, :, :] = w_two[keep]
        if not last:
            u_now, s_next, c_next = u_buf.at[k], s_buf.at[k + 1], c_buf.at[k + 1]
            shifted = []
            for src, dst, kept in (
                (u_now.at[(pl.ds(2, 2), *own[1:])], s_next.at[own], s_now.at[own]),
                (w_buf.at[k], c_next.at[own_c], c_now.at[own_c]),
            ):
                copy, index = remote(src, dst, device(later, y))
                stay = pltpu.make_async_copy(kept, dst, recv_sem.at[index])
                onward = m < nt - 1

                @pl.when(onward)
                def _(copy=copy):
                    copy.start()

                @pl.when(m == 0)
                def _(stay=stay):
                    stay.start()

                started.append((copy, onward))
                shifted.append(copy)
            u_halo = send_states(u_now)
            arrive(shifted[:1])
            s_halo = send_states(s_next)
            arrive(shifted[1:])
            c_halo = exchange(c_next, 2, near, 2, 2, 2, 4)

    out_in = move(o_buf, out_ref.at[0], out_to, y)
    arrive((out_in,))
    for copy, when in started:
        if when is None:
            copy.wait_send()
        else:

            @pl.when(when)
            def _(copy=copy):
                copy.wait_send()

    assert used[0] <= N_SEMS


def solution(mesh):
    dims = (mesh.shape["tm"], mesh.shape["gy"], mesh.shape["gx"])

    def shards(initial_state, slice_guess, feed_rate, kill_rate):
        buffers = [
            (ITERS, 2, 14, TALL, LANES),
            (ITERS, 2, 6, TALL, LANES),
            (ITERS - 1, 4, 14, TALL, LANES),
            (ITERS - 1, 2, 2, ROWS, LANES),
            (2, 12, TALL, LANES),
            (2, 10, TALL, LANES),
            (3, 12, TALL, LANES),
            (2, 12, TALL, LANES),
            (2, 10, TALL, LANES),
            (2, 12, TALL, LANES),
            (2, 12, TALL, LANES),
            (2, PLANES, ROWS, LANES),
        ]
        return pl.pallas_call(
            functools.partial(kernel, dims),
            out_shape=jax.ShapeDtypeStruct((1, 2, PLANES, ROWS, LANES), jnp.float32),
            in_specs=[pl.BlockSpec(memory_space=pl.ANY)] * 4,
            out_specs=pl.BlockSpec(memory_space=pl.ANY),
            scratch_shapes=[pltpu.VMEM(shape, jnp.float32) for shape in buffers]
            + [pltpu.SemaphoreType.DMA((N_SEMS,)), pltpu.SemaphoreType.DMA((N_SEMS,))],
            compiler_params=pltpu.CompilerParams(collective_id=0, has_side_effects=True),
        )(initial_state, slice_guess, feed_rate, kill_rate)

    in_specs = (
        P(None, "gy", "gx", None),
        P("tm", None, "gy", "gx", None),
        P("gy", "gx", None),
        P("gy", "gx", None),
    )
    out_specs = P("tm", None, "gy", "gx", None)
    return jax.shard_map(shards, mesh=mesh, in_specs=in_specs, out_specs=out_specs, check_vma=False)
```

```python
import functools

import jax
import jax.numpy as jnp
from jax import lax
from jax.experimental import pallas as pl
from jax.experimental.pallas import tpu as pltpu
from jax.sharding import PartitionSpec as P

ITERS = 3
DIFF = (0.2, 0.1)
HALF_STEP = 0.5
WEIGHTS = ((5.0 / 24.0, 8.0 / 24.0, -1.0 / 24.0), (-1.0 / 24.0, 8.0 / 24.0, 5.0 / 24.0))

PLANES, ROWS, LANES = 4, 16, 128
TALL, LOW, WINDOW, OWN = 40, 8, 24, 12
HALO = 5
SHIFT = 2
N_SEMS = 144


def kernel(dims, init_ref, guess_ref, feed_ref, kill_ref, out_ref,
           s_buf, c_buf, u_buf, w_buf, v1_buf, v2_buf, fk_buf, g0_buf, g1_buf, a0_buf, a1_buf, o_buf,
           send_sem, recv_sem):
    nt, ng, nx = dims
    chips = ng // 2
    blocks = nt // ng
    n, g, y = lax.axis_index("tm"), lax.axis_index("gy"), lax.axis_index("gx")

    def home_of(slice_at, tile):
        return slice_at, tile

    def role_of(slice_at, tile):
        along = (slice_at + SHIFT) % nt
        turned = (tile + 2 * (slice_at // (2 * blocks))) % ng
        return 2 * blocks * (turned // 2) + 2 * (along // ng) + turned % 2, along % ng

    def device(place, column):
        return {"tm": place[0], "gy": place[1], "gx": column}

    def is_me(place):
        return jnp.logical_and(place[0] == n, place[1] == g)

    across, block, core = n // (2 * blocks), (n // 2) % blocks, n % 2
    along = ng * block + g
    m = (along + nt - SHIFT) % nt
    t = (2 * across + core + ng - 2 * (m // (2 * blocks))) % ng

    s_to = role_of((n + 1) % nt, g)
    s_from = home_of((m + nt - 1) % nt, t)
    fk_along = g + nt - ng // 2 + ng * block + 2 * ((across + chips - g // 2) % chips) + core
    fk_to = role_of((fk_along + nt - SHIFT) % nt, g)
    fk_at = (along - t + ng // 2 + nt) % nt
    fk_from = (2 * blocks * ((t // 2 + (fk_at % ng) // 2) % chips) + 2 * (fk_at // ng) + fk_at % 2, t)
    out_to = home_of(m, t)
    out_from = role_of(n, g)
    later, earlier = role_of((m + 1) % nt, t), role_of((m + nt - 1) % nt, t)
    near = [(dx, dy) for dx in (-1, 0, 1) for dy in (-1, 0, 1) if (dx, dy) != (0, 0)]
    wide = near + [(-2, 0), (2, 0)]

    def neighbour(dx, dy):
        return device(role_of(m, (t + dx + ng) % ng), (y + dy + nx) % nx)

    barrier = pltpu.get_barrier_semaphore()
    partners = [device(place, y) for place in (s_from, fk_from, out_from, earlier, later)]
    partners += [neighbour(dx, dy) for dx, dy in wide]
    for partner in partners:
        pl.semaphore_signal(barrier, inc=1, device_id=partner, device_id_type=pl.DeviceIdType.MESH)
    pl.semaphore_wait(barrier, len(partners))

    used = [0]
    started = []

    def remote(src, dst, where):
        index = used[0]
        used[0] += 1
        return pltpu.make_async_remote_copy(
            src_ref=src, dst_ref=dst, send_sem=send_sem.at[index], recv_sem=recv_sem.at[index],
            device_id=where, device_id_type=pl.DeviceIdType.MESH), index

    def move(src, dst, place, column, when=None):
        copy, index = remote(src, dst, device(place, column))
        local = pltpu.make_async_copy(src, dst, recv_sem.at[index])
        away = jnp.logical_not(is_me(place))
        if when is not None:
            here = jnp.logical_and(when, is_me(place))
            away = jnp.logical_and(when, away)
        else:
            here = is_me(place)

        @pl.when(away)
        def _():
            copy.start()

        @pl.when(here)
        def _():
            local.start()

        started.append((copy, away))
        return copy

    def exchange(buf, first, fields, where, own_x, count, width_x, width_y, corner_x, corner_y):
        copies = []
        for dx, dy in where:
            corner = dx != 0 and dy != 0
            planes = count if dx == 0 else min(count, width_x - count * (abs(dx) - 1))
            rows_sent = ROWS if dy == 0 else width_y
            if corner:
                planes, rows_sent = corner_x, corner_y
            from_x = own_x + count - planes if dx > 0 else own_x
            from_y = OWN + ROWS - rows_sent if dy > 0 else OWN
            to_x, to_y = from_x - dx * count, from_y - dy * ROWS
            src = buf.at[pl.ds(first, fields), pl.ds(from_x, planes), pl.ds(from_y, rows_sent)]
            dst = buf.at[pl.ds(first, fields), pl.ds(to_x, planes), pl.ds(to_y, rows_sent)]
            copy, _ = remote(src, dst, neighbour(dx, dy))
            copy.start()
            started.append((copy, None))
            copies.append(copy)
        return copies

    def arrive(copies):
        for copy in copies:
            copy.wait_recv()

    own = (pl.ds(0, 2), pl.ds(HALO, PLANES), pl.ds(OWN, ROWS))
    own_c = (pl.ds(0, 2), pl.ds(2, 2), pl.ds(OWN, ROWS))

    fk_own = (pl.ds(4, PLANES), pl.ds(OWN, ROWS))
    first_s = s_buf.at[0]
    last_home = n == nt - 1
    mark = used[0]
    s_in = move(guess_ref.at[0], first_s.at[own], s_to, y, jnp.logical_not(last_home))
    used[0] = mark
    move(init_ref, first_s.at[own], s_to, y, last_home)
    feed_in = move(feed_ref, fk_buf.at[(0, *fk_own)], fk_to, y)
    kill_in = move(kill_ref, fk_buf.at[(1, *fk_own)], fk_to, y)

    row = lax.broadcasted_iota(jnp.int32, (WINDOW, LANES), 0)
    lane = lax.broadcasted_iota(jnp.int32, (WINDOW, LANES), 1)
    even_row, even_lane = row % 2 == 0, lane % 2 == 0

    def rows(by=0):
        return pl.ds(LOW + by, WINDOW)

    def turn(value, by, axis):
        size = value.shape[axis]
        return pltpu.roll(value, by % size, axis % value.ndim)

    def source(lap_u, lap_v, u, v, feed, both):
        reaction = u * v * v
        return lap_u - reaction + feed * (1.0 - u), lap_v + reaction - both * v

    def fine_rates(buf, first, at, feed_at, count):
        laps, mids = [], []
        for field in range(2):
            f = first + field
            mid = buf[f, pl.ds(at, count), rows(), :]
            total = buf[f, pl.ds(at - 1, count), rows(), :] + buf[f, pl.ds(at + 1, count), rows(), :]
            total = total + buf[f, pl.ds(at, count), rows(-1), :] + buf[f, pl.ds(at, count), rows(1), :]
            total = total + turn(mid, 1, -1) + turn(mid, -1, -1)
            laps.append(DIFF[field] * (total - 6.0 * mid))
            mids.append(mid)
        feed = fk_buf[0, pl.ds(feed_at, count), rows(), :]
        both = fk_buf[2, pl.ds(feed_at, count), rows(), :]
        return mids, source(laps[0], laps[1], mids[0], mids[1], feed, both)

    def pair_sum(value):
        value = value + jnp.where(even_row, turn(value, -1, -2), turn(value, 1, -2))
        return value + jnp.where(even_lane, turn(value, -1, -1), turn(value, 1, -1))

    def restrict(first, second):
        return 0.125 * pair_sum(first + second)

    def coarse_rates(below, mid, above, feed, both):
        laps = []
        for field in range(2):
            total = below[field] + above[field] + turn(mid[field], 2, -2) + turn(mid[field], -2, -2)
            total = total + turn(mid[field], 2, -1) + turn(mid[field], -2, -1)
            laps.append((0.25 * DIFF[field]) * (total - 6.0 * mid[field]))
        return source(laps[0], laps[1], mid[0], mid[1], feed, both)

    def send_states(buf, first, fields):
        return exchange(buf, first, fields, wide, HALO, PLANES, HALO, HALO, 4, 4)

    arrive((s_in,))
    s_halo = send_states(first_s, 0, 2)
    c_halo = []
    arrive((feed_in, kill_in))
    fk_halo = exchange(fk_buf, 0, 2, near, 4, PLANES, 4, 4, 3, 3)
    arrive(fk_halo)
    for p in range(0, 12, 2):
        both = fk_buf[0, pl.ds(p, 2), rows(), :] + fk_buf[1, pl.ds(p, 2), rows(), :]
        fk_buf[2, pl.ds(p, 2), rows(), :] = both
    coarse_feed, coarse_both = [], []
    for p in range(4):
        feed, kill = [restrict(fk_buf[f, 2 + 2 * p, rows(), :], fk_buf[f, 3 + 2 * p, rows(), :]) for f in range(2)]
        coarse_feed.append(feed)
        coarse_both.append(feed + kill)

    for k in range(ITERS):
        s_now, c_now = s_buf.at[k], c_buf.at[k]
        last = k == ITERS - 1
        if k > 0:
            u_old = u_buf.at[k - 1]
            arrive(u_halo)
            for p in range(0, 12, 2):
                _, one = fine_rates(u_old, 0, p + 1, p, 2)
                _, two = fine_rates(u_old, 2, p + 1, p, 2)
                for field in range(2):
                    zero = g0_buf[field, pl.ds(p, 2), rows(), :]
                    a0_buf[field, pl.ds(p, 2), rows(), :] = (
                        (WEIGHTS[0][0] - HALF_STEP) * zero + WEIGHTS[0][1] * one[field] + WEIGHTS[0][2] * two[field])
                    a1_buf[field, pl.ds(p, 2), rows(), :] = (
                        WEIGHTS[1][0] * zero + (WEIGHTS[1][1] - HALF_STEP) * one[field] + WEIGHTS[1][2] * two[field])
        arrive(s_halo)
        for p in range(0, 12, 2):
            mids, rates = fine_rates(s_now, 0, p + 1, p, 2)
            for field in range(2):
                node = mids[field] + HALF_STEP * rates[field]
                if k > 0:
                    node = node + a0_buf[field, pl.ds(p, 2), rows(), :]
                g0_buf[field, pl.ds(p, 2), rows(), :] = rates[field]
                v1_buf[field, pl.ds(p, 2), rows(), :] = node
        for p in range(0, 10, 2):
            mids, rates = fine_rates(v1_buf, 0, p + 1, p + 1, 2)
            for field in range(2):
                node = mids[field] + HALF_STEP * rates[field]
                if k > 0:
                    node = node + a1_buf[field, pl.ds(p + 1, 2), rows(), :]
                v2_buf[field, pl.ds(p, 2), rows(), :] = node
                g1_buf[field, pl.ds(p, 2), rows(), :] = rates[field]
        rest_s = [[restrict(s_now[f, 1 + 2 * p, rows(), :], s_now[f, 2 + 2 * p, rows(), :]) for f in range(2)]
                  for p in range(6)]
        if k == 0:
            coarse = rest_s
            for p in range(2, 4):
                for f in range(2):
                    c_now[f, p, rows(), :] = coarse[p][f]
        else:
            arrive(c_halo)
            coarse = [[c_now[f, p, rows(), :] for f in range(2)] for p in range(6)]
        w_one, late = [], []
        for p in range(4):
            _, two = fine_rates(v2_buf, 0, 2 * p + 1, 2 * p + 2, 2)
            rate_c = coarse_rates(coarse[p], coarse[p + 1], coarse[p + 2], coarse_feed[p], coarse_both[p])
            rate_s = coarse_rates(rest_s[p], rest_s[p + 1], rest_s[p + 2], coarse_feed[p], coarse_both[p])
            values, later_sums = [], []
            for f in range(2):
                zero = g0_buf[f, pl.ds(2 + 2 * p, 2), rows(), :]
                one = g1_buf[f, pl.ds(1 + 2 * p, 2), rows(), :]
                first, second = [w[0] * zero + w[1] * one + w[2] * two[f] for w in WEIGHTS]
                values.append(coarse[p + 1][f] + HALF_STEP * (rate_c[f] - rate_s[f]) + restrict(first[0], first[1]))
                later_sums.append(restrict(second[0], second[1]) if p in (1, 2) else None)
            w_one.append(values)
            late.append(later_sums)
        rest_v1 = [[restrict(v1_buf[f, 2 + 2 * p, rows(), :], v1_buf[f, 3 + 2 * p, rows(), :]) for f in range(2)]
                   for p in range(4)]
        keep = slice(OWN - LOW, OWN - LOW + ROWS)
        for p in (1, 2):
            rate_w = coarse_rates(w_one[p - 1], w_one[p], w_one[p + 1], coarse_feed[p], coarse_both[p])
            rate_v1 = coarse_rates(rest_v1[p - 1], rest_v1[p], rest_v1[p + 1], coarse_feed[p], coarse_both[p])
            for f in range(2):
                w_two = w_one[p][f] + HALF_STEP * (rate_w[f] - rate_v1[f]) + late[p][f]
                rest_v2 = restrict(v2_buf[f, 1 + 2 * p, rows(), :], v2_buf[f, 2 + 2 * p, rows(), :])
                for at in (2 * p - 2, 2 * p - 1):
                    two = v2_buf[f, 3 + at, rows(), :] + (w_two - rest_v2)
                    if last:
                        o_buf[f, at, :, :] = two[keep]
                    else:
                        one = v1_buf[f, 4 + at, rows(), :] + (w_one[p][f] - rest_v1[p][f])
                        u_buf[k, f, HALO + at, pl.ds(OWN, ROWS), :] = one[keep]
                        u_buf[k, 2 + f, HALO + at, pl.ds(OWN, ROWS), :] = two[keep]
                if not last:
                    w_buf[k, f, p - 1, :, :] = w_two[keep]
        if not last:
            u_now, s_next, c_next = u_buf.at[k], s_buf.at[k + 1], c_buf.at[k + 1]
            shifted = []
            for src, dst, kept in (
                (u_now.at[(pl.ds(2, 1), *own[1:])], s_next.at[(pl.ds(0, 1), *own[1:])], s_now.at[(pl.ds(0, 1), *own[1:])]),
                (u_now.at[(pl.ds(3, 1), *own[1:])], s_next.at[(pl.ds(1, 1), *own[1:])], s_now.at[(pl.ds(1, 1), *own[1:])]),
                (w_buf.at[k], c_next.at[own_c], c_now.at[own_c]),
            ):
                copy, index = remote(src, dst, device(later, y))
                stay = pltpu.make_async_copy(kept, dst, recv_sem.at[index])
                onward = m < nt - 1

                @pl.when(onward)
                def _(copy=copy):
                    copy.start()

                @pl.when(m == 0)
                def _(stay=stay):
                    stay.start()

                started.append((copy, onward))
                shifted.append(copy)
            u_halo = send_states(u_now, 0, 4)
            s_halo = []
            for field in range(2):
                arrive(shifted[field : field + 1])
                s_halo += send_states(s_next, field, 1)
            arrive(shifted[2:])
            c_halo = exchange(c_next, 0, 2, near, 2, 2, 2, 4, 1, 2)

    out_in = move(o_buf, out_ref.at[0], out_to, y)
    arrive((out_in,))
    for copy, when in started:
        if when is None:
            copy.wait_send()
        else:

            @pl.when(when)
            def _(copy=copy):
                copy.wait_send()

    assert used[0] <= N_SEMS


def solution(mesh):
    dims = (mesh.shape["tm"], mesh.shape["gy"], mesh.shape["gx"])

    def shards(initial_state, slice_guess, feed_rate, kill_rate):
        buffers = [
            (ITERS, 2, 14, TALL, LANES),
            (ITERS, 2, 6, TALL, LANES),
            (ITERS - 1, 4, 14, TALL, LANES),
            (ITERS - 1, 2, 2, ROWS, LANES),
            (2, 12, TALL, LANES),
            (2, 10, TALL, LANES),
            (3, 12, TALL, LANES),
            (2, 12, TALL, LANES),
            (2, 10, TALL, LANES),
            (2, 12, TALL, LANES),
            (2, 12, TALL, LANES),
            (2, PLANES, ROWS, LANES),
        ]
        return pl.pallas_call(
            functools.partial(kernel, dims),
            out_shape=jax.ShapeDtypeStruct((1, 2, PLANES, ROWS, LANES), jnp.float32),
            in_specs=[pl.BlockSpec(memory_space=pl.ANY)] * 4,
            out_specs=pl.BlockSpec(memory_space=pl.ANY),
            scratch_shapes=[pltpu.VMEM(shape, jnp.float32) for shape in buffers]
            + [pltpu.SemaphoreType.DMA((N_SEMS,)), pltpu.SemaphoreType.DMA((N_SEMS,))],
            compiler_params=pltpu.CompilerParams(collective_id=0, has_side_effects=True),
        )(initial_state, slice_guess, feed_rate, kill_rate)

    in_specs = (
        P(None, "gy", "gx", None),
        P("tm", None, "gy", "gx", None),
        P("gy", "gx", None),
        P("gy", "gx", None),
    )
    out_specs = P("tm", None, "gy", "gx", None)
    return jax.shard_map(shards, mesh=mesh, in_specs=in_specs, out_specs=out_specs, check_vma=False)
```

```python
import functools

import jax
import jax.numpy as jnp
from jax import lax
from jax.experimental import pallas as pl
from jax.experimental.pallas import tpu as pltpu
from jax.sharding import PartitionSpec as P

ITERS = 3
DIFF = (0.2, 0.1)
HALF_STEP = 0.5
WEIGHTS = ((5.0 / 24.0, 8.0 / 24.0, -1.0 / 24.0), (-1.0 / 24.0, 8.0 / 24.0, 5.0 / 24.0))

PLANES, ROWS, LANES = 4, 16, 128
TALL, LOW, WINDOW, OWN = 40, 8, 24, 12
HALO = 5
SHIFT = 2
N_SEMS = 160


def kernel(dims, init_ref, guess_ref, feed_ref, kill_ref, out_ref,
           s_buf, c_buf, u_buf, w_buf, v1_buf, v2_buf, fk_buf, g0_buf, g1_buf, a0_buf, a1_buf, o_buf,
           send_sem, recv_sem, home_sem):
    nt, ng, nx = dims
    chips = ng // 2
    blocks = nt // ng
    n, g, y = lax.axis_index("tm"), lax.axis_index("gy"), lax.axis_index("gx")

    def home_of(slice_at, tile):
        return slice_at, tile

    def role_of(slice_at, tile):
        along = (slice_at + SHIFT) % nt
        turned = (tile + 2 * (slice_at // (2 * blocks))) % ng
        return 2 * blocks * (turned // 2) + 2 * (along // ng) + turned % 2, along % ng

    def device(place, column):
        return {"tm": place[0], "gy": place[1], "gx": column}

    def is_me(place):
        return jnp.logical_and(place[0] == n, place[1] == g)

    across, block, core = n // (2 * blocks), (n // 2) % blocks, n % 2
    along = ng * block + g
    m = (along + nt - SHIFT) % nt
    t = (2 * across + core + ng - 2 * (m // (2 * blocks))) % ng

    s_to = role_of((n + 1) % nt, g)
    s_from = home_of((m + nt - 1) % nt, t)
    fk_along = g + nt - ng // 2 + ng * block + 2 * ((across + chips - g // 2) % chips) + core
    fk_to = role_of((fk_along + nt - SHIFT) % nt, g)
    fk_at = (along - t + ng // 2 + nt) % nt
    fk_from = (2 * blocks * ((t // 2 + (fk_at % ng) // 2) % chips) + 2 * (fk_at // ng) + fk_at % 2, t)
    out_to = home_of(m, t)
    later, earlier = role_of((m + 1) % nt, t), role_of((m + nt - 1) % nt, t)
    near = [(-1, -1), (-1, 1), (1, -1), (1, 1), (-1, 0), (1, 0), (0, -1), (0, 1)]
    wide = near[:6] + [(-2, 0), (2, 0)] + near[6:]

    def neighbour(dx, dy):
        return device(role_of(m, (t + dx + ng) % ng), (y + dy + nx) % nx)

    barrier = pltpu.get_barrier_semaphore()
    partners = [device(place, y) for place in (s_from, fk_from, earlier, later)]
    partners += [neighbour(dx, dy) for dx, dy in wide]
    for partner in partners:
        pl.semaphore_signal(barrier, inc=1, device_id=partner, device_id_type=pl.DeviceIdType.MESH)
    pl.semaphore_wait(barrier, len(partners))

    used = [0]
    started = []

    def remote(src, dst, where):
        index = used[0]
        used[0] += 1
        return pltpu.make_async_remote_copy(
            src_ref=src, dst_ref=dst, send_sem=send_sem.at[index], recv_sem=recv_sem.at[index],
            device_id=where, device_id_type=pl.DeviceIdType.MESH), index

    def move(src, dst, place, column, when=None):
        copy, index = remote(src, dst, device(place, column))
        local = pltpu.make_async_copy(src, dst, recv_sem.at[index])
        away = jnp.logical_not(is_me(place))
        if when is not None:
            here = jnp.logical_and(when, is_me(place))
            away = jnp.logical_and(when, away)
        else:
            here = is_me(place)

        @pl.when(away)
        def _():
            copy.start()

        @pl.when(here)
        def _():
            local.start()

        started.append((copy, away))
        return copy

    def exchange(buf, first, fields, where, own_x, count, width_x, width_y, corner_x, corner_y):
        copies = []
        for dx, dy in where:
            corner = dx != 0 and dy != 0
            planes = count if dx == 0 else min(count, width_x - count * (abs(dx) - 1))
            rows_sent = ROWS if dy == 0 else width_y
            if corner:
                planes, rows_sent = corner_x, corner_y
            from_x = own_x + count - planes if dx > 0 else own_x
            from_y = OWN + ROWS - rows_sent if dy > 0 else OWN
            to_x, to_y = from_x - dx * count, from_y - dy * ROWS
            src = buf.at[pl.ds(first, fields), pl.ds(from_x, planes), pl.ds(from_y, rows_sent)]
            dst = buf.at[pl.ds(first, fields), pl.ds(to_x, planes), pl.ds(to_y, rows_sent)]
            copy, _ = remote(src, dst, neighbour(dx, dy))
            copy.start()
            started.append((copy, None))
            copies.append(copy)
        return copies

    def arrive(copies):
        for copy in copies:
            copy.wait_recv()

    own = (pl.ds(0, 2), pl.ds(HALO, PLANES), pl.ds(OWN, ROWS))
    own_c = (pl.ds(0, 2), pl.ds(2, 2), pl.ds(OWN, ROWS))

    fk_own = (pl.ds(4, PLANES), pl.ds(OWN, ROWS))
    first_s = s_buf.at[0]
    last_home = n == nt - 1
    s_in = []
    for field in range(2):
        part = (field, *own[1:])
        mark = used[0]
        s_in.append(move(guess_ref.at[0, field], first_s.at[part], s_to, y, jnp.logical_not(last_home)))
        used[0] = mark
        move(init_ref.at[field], first_s.at[part], s_to, y, last_home)
    feed_in = move(feed_ref, fk_buf.at[(0, *fk_own)], fk_to, y)
    kill_in = move(kill_ref, fk_buf.at[(1, *fk_own)], fk_to, y)

    row = lax.broadcasted_iota(jnp.int32, (WINDOW, LANES), 0)
    lane = lax.broadcasted_iota(jnp.int32, (WINDOW, LANES), 1)
    even_row, even_lane = row % 2 == 0, lane % 2 == 0

    def rows(by=0):
        return pl.ds(LOW + by, WINDOW)

    def turn(value, by, axis):
        size = value.shape[axis]
        return pltpu.roll(value, by % size, axis % value.ndim)

    def source(lap_u, lap_v, u, v, feed, both):
        reaction = u * v * v
        return lap_u - reaction + feed * (1.0 - u), lap_v + reaction - both * v

    def fine_rates(buf, first, at, feed_at, count):
        laps, mids = [], []
        for field in range(2):
            f = first + field
            mid = buf[f, pl.ds(at, count), rows(), :]
            total = buf[f, pl.ds(at - 1, count), rows(), :] + buf[f, pl.ds(at + 1, count), rows(), :]
            total = total + buf[f, pl.ds(at, count), rows(-1), :] + buf[f, pl.ds(at, count), rows(1), :]
            total = total + turn(mid, 1, -1) + turn(mid, -1, -1)
            laps.append(DIFF[field] * (total - 6.0 * mid))
            mids.append(mid)
        feed = fk_buf[0, pl.ds(feed_at, count), rows(), :]
        both = fk_buf[2, pl.ds(feed_at, count), rows(), :]
        return mids, source(laps[0], laps[1], mids[0], mids[1], feed, both)

    def pair_sum(value):
        value = value + jnp.where(even_row, turn(value, -1, -2), turn(value, 1, -2))
        return value + jnp.where(even_lane, turn(value, -1, -1), turn(value, 1, -1))

    def restrict(first, second):
        return 0.125 * pair_sum(first + second)

    def coarse_rates(below, mid, above, feed, both):
        laps = []
        for field in range(2):
            total = below[field] + above[field] + turn(mid[field], 2, -2) + turn(mid[field], -2, -2)
            total = total + turn(mid[field], 2, -1) + turn(mid[field], -2, -1)
            laps.append((0.25 * DIFF[field]) * (total - 6.0 * mid[field]))
        return source(laps[0], laps[1], mid[0], mid[1], feed, both)

    def send_states(buf, first, fields):
        return exchange(buf, first, fields, wide, HALO, PLANES, HALO, HALO, 4, 4)

    s_halo, c_halo, fk_halo = [], [], []
    for field in range(2):
        arrive((s_in[field],))
        s_halo += send_states(first_s, field, 1)
    pl.semaphore_signal(home_sem, inc=1, device_id=device(earlier, y), device_id_type=pl.DeviceIdType.MESH)
    for field, moved in enumerate((feed_in, kill_in)):
        arrive((moved,))
        fk_halo += exchange(fk_buf, field, 1, near, 4, PLANES, 4, 4, 3, 3)
    arrive(fk_halo)
    for p in range(0, 12, 2):
        both = fk_buf[0, pl.ds(p, 2), rows(), :] + fk_buf[1, pl.ds(p, 2), rows(), :]
        fk_buf[2, pl.ds(p, 2), rows(), :] = both
    coarse_feed, coarse_both = [], []
    for p in range(4):
        feed, kill = [restrict(fk_buf[f, 2 + 2 * p, rows(), :], fk_buf[f, 3 + 2 * p, rows(), :]) for f in range(2)]
        coarse_feed.append(feed)
        coarse_both.append(feed + kill)

    for k in range(ITERS):
        s_now, c_now = s_buf.at[k], c_buf.at[k]
        last = k == ITERS - 1
        if k > 0:
            u_old = u_buf.at[k - 1]
            arrive(u_halo)
            for p in range(0, 12, 2):
                _, one = fine_rates(u_old, 0, p + 1, p, 2)
                _, two = fine_rates(u_old, 2, p + 1, p, 2)
                for field in range(2):
                    zero = g0_buf[field, pl.ds(p, 2), rows(), :]
                    a0_buf[field, pl.ds(p, 2), rows(), :] = (
                        (WEIGHTS[0][0] - HALF_STEP) * zero + WEIGHTS[0][1] * one[field] + WEIGHTS[0][2] * two[field])
                    a1_buf[field, pl.ds(p, 2), rows(), :] = (
                        WEIGHTS[1][0] * zero + (WEIGHTS[1][1] - HALF_STEP) * one[field] + WEIGHTS[1][2] * two[field])
        arrive(s_halo)
        for p in range(0, 12, 2):
            mids, rates = fine_rates(s_now, 0, p + 1, p, 2)
            for field in range(2):
                node = mids[field] + HALF_STEP * rates[field]
                if k > 0:
                    node = node + a0_buf[field, pl.ds(p, 2), rows(), :]
                g0_buf[field, pl.ds(p, 2), rows(), :] = rates[field]
                v1_buf[field, pl.ds(p, 2), rows(), :] = node
        for p in range(0, 10, 2):
            mids, rates = fine_rates(v1_buf, 0, p + 1, p + 1, 2)
            for field in range(2):
                node = mids[field] + HALF_STEP * rates[field]
                if k > 0:
                    node = node + a1_buf[field, pl.ds(p + 1, 2), rows(), :]
                v2_buf[field, pl.ds(p, 2), rows(), :] = node
                g1_buf[field, pl.ds(p, 2), rows(), :] = rates[field]
        rest_s = [[restrict(s_now[f, 1 + 2 * p, rows(), :], s_now[f, 2 + 2 * p, rows(), :]) for f in range(2)]
                  for p in range(6)]
        if k == 0:
            coarse = rest_s
            for p in range(2, 4):
                for f in range(2):
                    c_now[f, p, rows(), :] = coarse[p][f]
        else:
            arrive(c_halo)
            coarse = [[c_now[f, p, rows(), :] for f in range(2)] for p in range(6)]
        w_one, late = [], []
        for p in range(4):
            _, two = fine_rates(v2_buf, 0, 2 * p + 1, 2 * p + 2, 2)
            rate_c = coarse_rates(coarse[p], coarse[p + 1], coarse[p + 2], coarse_feed[p], coarse_both[p])
            rate_s = coarse_rates(rest_s[p], rest_s[p + 1], rest_s[p + 2], coarse_feed[p], coarse_both[p])
            values, later_sums = [], []
            for f in range(2):
                zero = g0_buf[f, pl.ds(2 + 2 * p, 2), rows(), :]
                one = g1_buf[f, pl.ds(1 + 2 * p, 2), rows(), :]
                first, second = [w[0] * zero + w[1] * one + w[2] * two[f] for w in WEIGHTS]
                values.append(coarse[p + 1][f] + HALF_STEP * (rate_c[f] - rate_s[f]) + restrict(first[0], first[1]))
                later_sums.append(restrict(second[0], second[1]) if p in (1, 2) else None)
            w_one.append(values)
            late.append(later_sums)
        rest_v1 = [[restrict(v1_buf[f, 2 + 2 * p, rows(), :], v1_buf[f, 3 + 2 * p, rows(), :]) for f in range(2)]
                   for p in range(4)]
        keep = slice(OWN - LOW, OWN - LOW + ROWS)
        for p in (1, 2):
            rate_w = coarse_rates(w_one[p - 1], w_one[p], w_one[p + 1], coarse_feed[p], coarse_both[p])
            rate_v1 = coarse_rates(rest_v1[p - 1], rest_v1[p], rest_v1[p + 1], coarse_feed[p], coarse_both[p])
            for f in range(2):
                w_two = w_one[p][f] + HALF_STEP * (rate_w[f] - rate_v1[f]) + late[p][f]
                rest_v2 = restrict(v2_buf[f, 1 + 2 * p, rows(), :], v2_buf[f, 2 + 2 * p, rows(), :])
                for at in (2 * p - 2, 2 * p - 1):
                    two = v2_buf[f, 3 + at, rows(), :] + (w_two - rest_v2)
                    if last:
                        o_buf[f, at, :, :] = two[keep]
                    else:
                        one = v1_buf[f, 4 + at, rows(), :] + (w_one[p][f] - rest_v1[p][f])
                        u_buf[k, f, HALO + at, pl.ds(OWN, ROWS), :] = one[keep]
                        u_buf[k, 2 + f, HALO + at, pl.ds(OWN, ROWS), :] = two[keep]
                if not last:
                    w_buf[k, f, p - 1, :, :] = w_two[keep]
        if not last:
            u_now, s_next, c_next = u_buf.at[k], s_buf.at[k + 1], c_buf.at[k + 1]
            shifted = []
            for src, dst, kept in (
                (u_now.at[(pl.ds(2, 1), *own[1:])], s_next.at[(pl.ds(0, 1), *own[1:])], s_now.at[(pl.ds(0, 1), *own[1:])]),
                (u_now.at[(pl.ds(3, 1), *own[1:])], s_next.at[(pl.ds(1, 1), *own[1:])], s_now.at[(pl.ds(1, 1), *own[1:])]),
                (w_buf.at[k], c_next.at[own_c], c_now.at[own_c]),
            ):
                copy, index = remote(src, dst, device(later, y))
                stay = pltpu.make_async_copy(kept, dst, recv_sem.at[index])
                onward = m < nt - 1

                @pl.when(onward)
                def _(copy=copy):
                    copy.start()

                @pl.when(m == 0)
                def _(stay=stay):
                    stay.start()

                started.append((copy, onward))
                shifted.append(copy)
            u_halo = send_states(u_now, 0, 4)
            s_halo = []
            for field in range(2):
                arrive(shifted[field : field + 1])
                s_halo += send_states(s_next, field, 1)
            arrive(shifted[2:])
            c_halo = exchange(c_next, 0, 2, near, 2, 2, 2, 4, 1, 2)

    pl.semaphore_wait(home_sem, 1)
    out_in = move(o_buf, out_ref.at[0], out_to, y)
    arrive((out_in,))
    for copy, when in started:
        if when is None:
            copy.wait_send()
        else:

            @pl.when(when)
            def _(copy=copy):
                copy.wait_send()

    assert used[0] <= N_SEMS


def solution(mesh):
    dims = (mesh.shape["tm"], mesh.shape["gy"], mesh.shape["gx"])

    def shards(initial_state, slice_guess, feed_rate, kill_rate):
        buffers = [
            (ITERS, 2, 14, TALL, LANES),
            (ITERS, 2, 6, TALL, LANES),
            (ITERS - 1, 4, 14, TALL, LANES),
            (ITERS - 1, 2, 2, ROWS, LANES),
            (2, 12, TALL, LANES),
            (2, 10, TALL, LANES),
            (3, 12, TALL, LANES),
            (2, 12, TALL, LANES),
            (2, 10, TALL, LANES),
            (2, 12, TALL, LANES),
            (2, 12, TALL, LANES),
            (2, PLANES, ROWS, LANES),
        ]
        return pl.pallas_call(
            functools.partial(kernel, dims),
            out_shape=jax.ShapeDtypeStruct((1, 2, PLANES, ROWS, LANES), jnp.float32),
            in_specs=[pl.BlockSpec(memory_space=pl.ANY)] * 4,
            out_specs=pl.BlockSpec(memory_space=pl.ANY),
            scratch_shapes=[pltpu.VMEM(shape, jnp.float32) for shape in buffers]
            + [pltpu.SemaphoreType.DMA((N_SEMS,)), pltpu.SemaphoreType.DMA((N_SEMS,)), pltpu.SemaphoreType.REGULAR],
            compiler_params=pltpu.CompilerParams(collective_id=0, has_side_effects=True),
        )(initial_state, slice_guess, feed_rate, kill_rate)

    in_specs = (
        P(None, "gy", "gx", None),
        P("tm", None, "gy", "gx", None),
        P("gy", "gx", None),
        P("gy", "gx", None),
    )
    out_specs = P("tm", None, "gy", "gx", None)
    return jax.shard_map(shards, mesh=mesh, in_specs=in_specs, out_specs=out_specs, check_vma=False)
```

```python
import functools

import jax
import jax.numpy as jnp
from jax import lax
from jax.experimental import pallas as pl
from jax.experimental.pallas import tpu as pltpu
from jax.sharding import PartitionSpec as P

ITERS = 3
DIFF = (0.2, 0.1)
HALF_STEP = 0.5
WEIGHTS = ((5.0 / 24.0, 8.0 / 24.0, -1.0 / 24.0), (-1.0 / 24.0, 8.0 / 24.0, 5.0 / 24.0))

PLANES, ROWS, LANES = 4, 16, 128
TALL, LOW, WINDOW, OWN = 40, 8, 24, 12
HALO = 5
SHIFT = 8
N_SEMS = 160


def kernel(dims, init_ref, guess_ref, feed_ref, kill_ref, out_ref,
           s_buf, c_buf, u_buf, w_buf, v1_buf, v2_buf, fk_buf, g0_buf, g1_buf, a0_buf, a1_buf, o_buf,
           send_sem, recv_sem, home_sem):
    nt, ng, nx = dims
    chips = ng // 2
    blocks = nt // ng
    n, g, y = lax.axis_index("tm"), lax.axis_index("gy"), lax.axis_index("gx")

    def home_of(slice_at, tile):
        return slice_at, tile

    def role_of(slice_at, tile):
        along = (slice_at + SHIFT) % nt
        turned = tile
        return 2 * blocks * (turned // 2) + 2 * (along // ng) + turned % 2, along % ng

    def device(place, column):
        return {"tm": place[0], "gy": place[1], "gx": column}

    def is_me(place):
        return jnp.logical_and(place[0] == n, place[1] == g)

    across, block, core = n // (2 * blocks), (n // 2) % blocks, n % 2
    along = ng * block + g
    m = (along + nt - SHIFT) % nt
    t = (2 * across + core + ng) % ng

    s_to = role_of((n + 1) % nt, g)
    s_from = home_of((m + nt - 1) % nt, t)
    fk_along = g + nt - ng // 2 + ng * block + 2 * ((across + chips - g // 2) % chips) + core
    fk_to = role_of((fk_along + nt - SHIFT) % nt, g)
    fk_at = (along - t + ng // 2 + nt) % nt
    fk_from = (2 * blocks * ((t // 2 + (fk_at % ng) // 2) % chips) + 2 * (fk_at // ng) + fk_at % 2, t)
    out_to = home_of(m, t)
    later, earlier = role_of((m + 1) % nt, t), role_of((m + nt - 1) % nt, t)
    near = [(-1, -1), (-1, 1), (1, -1), (1, 1), (-1, 0), (1, 0), (0, -1), (0, 1)]
    wide = near[:6] + [(-2, 0), (2, 0)] + near[6:]

    def neighbour(dx, dy, ahead=0):
        return device(role_of((m + ahead + nt) % nt, (t + dx + ng) % ng), (y + dy + nx) % nx)

    barrier = pltpu.get_barrier_semaphore()
    partners = [device(place, y) for place in (s_from, fk_from, later)]
    partners += [neighbour(dx, dy) for dx, dy in wide] + [neighbour(dx, dy, -1) for dx, dy in [(0, 0)] + near]
    for partner in partners:
        pl.semaphore_signal(barrier, inc=1, device_id=partner, device_id_type=pl.DeviceIdType.MESH)
    pl.semaphore_wait(barrier, len(partners))

    used = [0]
    started = []

    def remote(src, dst, where):
        index = used[0]
        used[0] += 1
        return pltpu.make_async_remote_copy(
            src_ref=src, dst_ref=dst, send_sem=send_sem.at[index], recv_sem=recv_sem.at[index],
            device_id=where, device_id_type=pl.DeviceIdType.MESH), index

    def move(src, dst, place, column, when=None):
        copy, index = remote(src, dst, device(place, column))
        local = pltpu.make_async_copy(src, dst, recv_sem.at[index])
        away = jnp.logical_not(is_me(place))
        if when is not None:
            here = jnp.logical_and(when, is_me(place))
            away = jnp.logical_and(when, away)
        else:
            here = is_me(place)

        @pl.when(away)
        def _():
            copy.start()

        @pl.when(here)
        def _():
            local.start()

        started.append((copy, away))
        return copy

    def piece(dx, dy, own_x, count, width_x, width_y, corner_x, corner_y):
        planes = count if dx == 0 else min(count, width_x - count * (abs(dx) - 1))
        rows_sent = ROWS if dy == 0 else width_y
        if dx != 0 and dy != 0:
            planes, rows_sent = corner_x, corner_y
        from_x = own_x + count - planes if dx > 0 else own_x
        from_y = OWN + ROWS - rows_sent if dy > 0 else OWN
        to_x, to_y = from_x - dx * count, from_y - dy * ROWS
        return (pl.ds(from_x, planes), pl.ds(from_y, rows_sent)), (pl.ds(to_x, planes), pl.ds(to_y, rows_sent))

    def exchange(buf, first, fields, where, *sizes):
        copies = []
        for dx, dy in where:
            src, dst = piece(dx, dy, *sizes)
            copy, _ = remote(buf.at[(pl.ds(first, fields), *src)], buf.at[(pl.ds(first, fields), *dst)], neighbour(dx, dy))
            copy.start()
            started.append((copy, None))
            copies.append(copy)
        return copies

    onward = m < nt - 1

    def hand_on(src, dst, kept, dx=0, dy=0):
        copy, index = remote(src, dst, neighbour(dx, dy, 1))
        stay = pltpu.make_async_copy(kept, dst, recv_sem.at[index])

        @pl.when(onward)
        def _():
            copy.start()

        @pl.when(m == 0)
        def _():
            stay.start()

        started.append((copy, onward))
        return copy

    def arrive(copies):
        for copy in copies:
            copy.wait_recv()

    own = (pl.ds(0, 2), pl.ds(HALO, PLANES), pl.ds(OWN, ROWS))
    s_sizes = (HALO, PLANES, HALO, HALO, 4, 4)

    fk_own = (pl.ds(4, PLANES), pl.ds(OWN, ROWS))
    first_s = s_buf.at[0]
    last_home = n == nt - 1
    s_in = []
    for field in range(2):
        part = (field, *own[1:])
        mark = used[0]
        s_in.append(move(guess_ref.at[0, field], first_s.at[part], s_to, y, jnp.logical_not(last_home)))
        used[0] = mark
        move(init_ref.at[field], first_s.at[part], s_to, y, last_home)
    feed_in = move(feed_ref, fk_buf.at[(0, *fk_own)], fk_to, y)
    kill_in = move(kill_ref, fk_buf.at[(1, *fk_own)], fk_to, y)

    row = lax.broadcasted_iota(jnp.int32, (WINDOW, LANES), 0)
    lane = lax.broadcasted_iota(jnp.int32, (WINDOW, LANES), 1)
    even_row, even_lane = row % 2 == 0, lane % 2 == 0

    def rows(by=0):
        return pl.ds(LOW + by, WINDOW)

    def turn(value, by, axis):
        size = value.shape[axis]
        return pltpu.roll(value, by % size, axis % value.ndim)

    def source(lap_u, lap_v, u, v, feed, both):
        reaction = u * v * v
        return lap_u - reaction + feed * (1.0 - u), lap_v + reaction - both * v

    def fine_rates(buf, first, at, feed_at, count):
        laps, mids = [], []
        for field in range(2):
            f = first + field
            mid = buf[f, pl.ds(at, count), rows(), :]
            total = buf[f, pl.ds(at - 1, count), rows(), :] + buf[f, pl.ds(at + 1, count), rows(), :]
            total = total + buf[f, pl.ds(at, count), rows(-1), :] + buf[f, pl.ds(at, count), rows(1), :]
            total = total + turn(mid, 1, -1) + turn(mid, -1, -1)
            laps.append(DIFF[field] * (total - 6.0 * mid))
            mids.append(mid)
        feed = fk_buf[0, pl.ds(feed_at, count), rows(), :]
        both = fk_buf[2, pl.ds(feed_at, count), rows(), :]
        return mids, source(laps[0], laps[1], mids[0], mids[1], feed, both)

    def pair_sum(value):
        value = value + jnp.where(even_row, turn(value, -1, -2), turn(value, 1, -2))
        return value + jnp.where(even_lane, turn(value, -1, -1), turn(value, 1, -1))

    def restrict(first, second):
        return 0.125 * pair_sum(first + second)

    def coarse_rates(below, mid, above, feed, both):
        laps = []
        for field in range(2):
            total = below[field] + above[field] + turn(mid[field], 2, -2) + turn(mid[field], -2, -2)
            total = total + turn(mid[field], 2, -1) + turn(mid[field], -2, -1)
            laps.append((0.25 * DIFF[field]) * (total - 6.0 * mid[field]))
        return source(laps[0], laps[1], mid[0], mid[1], feed, both)

    def pack(planes):
        mixed = [jnp.where(even_lane, plane[0], plane[1]) for plane in planes]
        return jnp.where(even_row, mixed[0], mixed[1])

    def unpack(packed):
        planes = [jnp.where(even_row, packed, turn(packed, 1, -2)), jnp.where(even_row, turn(packed, -1, -2), packed)]
        return [[jnp.where(even_lane, plane, turn(plane, 1, -1)), jnp.where(even_lane, turn(plane, -1, -1), plane)]
                for plane in planes]

    def send_states(buf, first, fields):
        return exchange(buf, first, fields, wide, *s_sizes)

    s_halo, c_halo, fk_halo = [], [], []
    for field in range(2):
        arrive((s_in[field],))
        s_halo += send_states(first_s, field, 1)
    pl.semaphore_signal(home_sem, inc=1, device_id=device(earlier, y), device_id_type=pl.DeviceIdType.MESH)
    for field, moved in enumerate((feed_in, kill_in)):
        arrive((moved,))
        fk_halo += exchange(fk_buf, field, 1, near, 4, PLANES, 4, 4, 3, 3)
    arrive(fk_halo)
    for p in range(0, 12, 2):
        both = fk_buf[0, pl.ds(p, 2), rows(), :] + fk_buf[1, pl.ds(p, 2), rows(), :]
        fk_buf[2, pl.ds(p, 2), rows(), :] = both
    coarse_feed, coarse_both = [], []
    for p in range(4):
        feed, kill = [restrict(fk_buf[f, 2 + 2 * p, rows(), :], fk_buf[f, 3 + 2 * p, rows(), :]) for f in range(2)]
        coarse_feed.append(feed)
        coarse_both.append(feed + kill)

    for k in range(ITERS):
        s_now, c_now = s_buf.at[k], c_buf.at[k]
        last = k == ITERS - 1
        if k > 0:
            u_old = u_buf.at[k - 1]
            arrive(u_halo)
            for p in range(0, 12, 2):
                _, one = fine_rates(u_old, 0, p + 1, p, 2)
                _, two = fine_rates(u_old, 2, p + 1, p, 2)
                for field in range(2):
                    zero = g0_buf[field, pl.ds(p, 2), rows(), :]
                    a0_buf[field, pl.ds(p, 2), rows(), :] = (
                        (WEIGHTS[0][0] - HALF_STEP) * zero + WEIGHTS[0][1] * one[field] + WEIGHTS[0][2] * two[field])
                    a1_buf[field, pl.ds(p, 2), rows(), :] = (
                        WEIGHTS[1][0] * zero + (WEIGHTS[1][1] - HALF_STEP) * one[field] + WEIGHTS[1][2] * two[field])
        arrive(s_halo)
        for p in range(0, 12, 2):
            mids, rates = fine_rates(s_now, 0, p + 1, p, 2)
            for field in range(2):
                node = mids[field] + HALF_STEP * rates[field]
                if k > 0:
                    node = node + a0_buf[field, pl.ds(p, 2), rows(), :]
                g0_buf[field, pl.ds(p, 2), rows(), :] = rates[field]
                v1_buf[field, pl.ds(p, 2), rows(), :] = node
        for p in range(0, 10, 2):
            mids, rates = fine_rates(v1_buf, 0, p + 1, p + 1, 2)
            for field in range(2):
                node = mids[field] + HALF_STEP * rates[field]
                if k > 0:
                    node = node + a1_buf[field, pl.ds(p + 1, 2), rows(), :]
                v2_buf[field, pl.ds(p, 2), rows(), :] = node
                g1_buf[field, pl.ds(p, 2), rows(), :] = rates[field]
        rest_s = [[restrict(s_now[f, 1 + 2 * p, rows(), :], s_now[f, 2 + 2 * p, rows(), :]) for f in range(2)]
                  for p in range(6)]
        if k == 0:
            coarse = rest_s
            for p in range(3):
                c_now[p, rows(), :] = pack(coarse[2 * p : 2 * p + 2])
        else:
            arrive(c_halo)
            coarse = [plane for p in range(3) for plane in unpack(c_now[p, rows(), :])]
        w_one, late = [], []
        for p in range(4):
            _, two = fine_rates(v2_buf, 0, 2 * p + 1, 2 * p + 2, 2)
            rate_c = coarse_rates(coarse[p], coarse[p + 1], coarse[p + 2], coarse_feed[p], coarse_both[p])
            rate_s = coarse_rates(rest_s[p], rest_s[p + 1], rest_s[p + 2], coarse_feed[p], coarse_both[p])
            values, later_sums = [], []
            for f in range(2):
                zero = g0_buf[f, pl.ds(2 + 2 * p, 2), rows(), :]
                one = g1_buf[f, pl.ds(1 + 2 * p, 2), rows(), :]
                first, second = [w[0] * zero + w[1] * one + w[2] * two[f] for w in WEIGHTS]
                values.append(coarse[p + 1][f] + HALF_STEP * (rate_c[f] - rate_s[f]) + restrict(first[0], first[1]))
                later_sums.append(restrict(second[0], second[1]) if p in (1, 2) else None)
            w_one.append(values)
            late.append(later_sums)
        rest_v1 = [[restrict(v1_buf[f, 2 + 2 * p, rows(), :], v1_buf[f, 3 + 2 * p, rows(), :]) for f in range(2)]
                   for p in range(4)]
        keep = slice(OWN - LOW, OWN - LOW + ROWS)
        w_two = []
        for p in (1, 2):
            w_two.append([])
            rate_w = coarse_rates(w_one[p - 1], w_one[p], w_one[p + 1], coarse_feed[p], coarse_both[p])
            rate_v1 = coarse_rates(rest_v1[p - 1], rest_v1[p], rest_v1[p + 1], coarse_feed[p], coarse_both[p])
            for f in range(2):
                w_end = w_one[p][f] + HALF_STEP * (rate_w[f] - rate_v1[f]) + late[p][f]
                w_two[-1].append(w_end)
                rest_v2 = restrict(v2_buf[f, 1 + 2 * p, rows(), :], v2_buf[f, 2 + 2 * p, rows(), :])
                for at in (2 * p - 2, 2 * p - 1):
                    two = v2_buf[f, 3 + at, rows(), :] + (w_end - rest_v2)
                    if last:
                        o_buf[f, at, :, :] = two[keep]
                    else:
                        one = v1_buf[f, 4 + at, rows(), :] + (w_one[p][f] - rest_v1[p][f])
                        u_buf[k, f, HALO + at, pl.ds(OWN, ROWS), :] = one[keep]
                        u_buf[k, 2 + f, HALO + at, pl.ds(OWN, ROWS), :] = two[keep]
        if not last:
            w_buf[k, :, :] = pack(w_two)[keep]
            u_now, s_next, c_next = u_buf.at[k], s_buf.at[k + 1], c_buf.at[k + 1]
            shifted = [
                hand_on(u_now.at[(2 + f, *own[1:])], s_next.at[(f, *own[1:])], s_now.at[(f, *own[1:])]) for f in range(2)
            ]
            s_halo = []
            for dx, dy in near:
                if dx != 0 and dy != 0:
                    src, dst = piece(dx, dy, *s_sizes)
                    src, dst = (pl.ds(2, 2), *src), (pl.ds(0, 2), *dst)
                    s_halo.append(hand_on(u_now.at[src], s_next.at[dst], s_now.at[dst], dx, dy))
            c_halo = []
            for dx, dy in [(0, 0)] + near:
                sent = ROWS if dy == 0 else 4
                from_y = ROWS - sent if dy > 0 else 0
                src, dst = pl.ds(from_y, sent), (1 - dx, pl.ds(OWN + from_y - dy * ROWS, sent))
                c_halo.append(hand_on(w_buf.at[k, src], c_next.at[dst], c_now.at[dst], dx, dy))
            u_halo = send_states(u_now, 0, 4)
            for field in range(2):
                arrive(shifted[field : field + 1])
                s_halo += exchange(s_next, field, 1, wide[4:], *s_sizes)

    pl.semaphore_wait(home_sem, 1)
    out_in = move(o_buf, out_ref.at[0], out_to, y)
    arrive((out_in,))
    for copy, when in started:
        if when is None:
            copy.wait_send()
        else:

            @pl.when(when)
            def _(copy=copy):
                copy.wait_send()

    assert used[0] <= N_SEMS


def solution(mesh):
    dims = (mesh.shape["tm"], mesh.shape["gy"], mesh.shape["gx"])

    def shards(initial_state, slice_guess, feed_rate, kill_rate):
        buffers = [
            (ITERS, 2, 14, TALL, LANES),
            (ITERS, 3, TALL, LANES),
            (ITERS - 1, 4, 14, TALL, LANES),
            (ITERS - 1, ROWS, LANES),
            (2, 12, TALL, LANES),
            (2, 10, TALL, LANES),
            (3, 12, TALL, LANES),
            (2, 12, TALL, LANES),
            (2, 10, TALL, LANES),
            (2, 12, TALL, LANES),
            (2, 12, TALL, LANES),
            (2, PLANES, ROWS, LANES),
        ]
        return pl.pallas_call(
            functools.partial(kernel, dims),
            out_shape=jax.ShapeDtypeStruct((1, 2, PLANES, ROWS, LANES), jnp.float32),
            in_specs=[pl.BlockSpec(memory_space=pl.ANY)] * 4,
            out_specs=pl.BlockSpec(memory_space=pl.ANY),
            scratch_shapes=[pltpu.VMEM(shape, jnp.float32) for shape in buffers]
            + [pltpu.SemaphoreType.DMA((N_SEMS,)), pltpu.SemaphoreType.DMA((N_SEMS,)), pltpu.SemaphoreType.REGULAR],
            compiler_params=pltpu.CompilerParams(collective_id=0, has_side_effects=True),
        )(initial_state, slice_guess, feed_rate, kill_rate)

    in_specs = (
        P(None, "gy", "gx", None),
        P("tm", None, "gy", "gx", None),
        P("gy", "gx", None),
        P("gy", "gx", None),
    )
    out_specs = P("tm", None, "gy", "gx", None)
    return jax.shard_map(shards, mesh=mesh, in_specs=in_specs, out_specs=out_specs, check_vma=False)
```

```python
import functools

import jax
import jax.numpy as jnp
from jax import lax
from jax.experimental import pallas as pl
from jax.experimental.pallas import tpu as pltpu
from jax.sharding import PartitionSpec as P

ITERS = 3
DIFF = (0.2, 0.1)
HALF_STEP = 0.5
WEIGHTS = ((5.0 / 24.0, 8.0 / 24.0, -1.0 / 24.0), (-1.0 / 24.0, 8.0 / 24.0, 5.0 / 24.0))

PLANES, ROWS, LANES = 4, 16, 128
TALL, LOW, WINDOW, OWN = 40, 8, 24, 12
HALO = 5
SHIFT = 9
N_SEMS = 160


def kernel(dims, init_ref, guess_ref, feed_ref, kill_ref, out_ref,
           s_buf, c_buf, u_buf, w_buf, v1_buf, v2_buf, fk_buf, g0_buf, g1_buf, a0_buf, a1_buf, o_buf,
           send_sem, recv_sem, home_sem):
    nt, ng, nx = dims
    chips = ng // 2
    blocks = nt // ng
    n, g, y = lax.axis_index("tm"), lax.axis_index("gy"), lax.axis_index("gx")

    def home_of(slice_at, tile):
        return slice_at, tile

    def role_of(slice_at, tile):
        along = (slice_at + SHIFT) % nt
        turned = tile
        return 2 * blocks * (turned // 2) + 2 * (along // ng) + turned % 2, along % ng

    def device(place, column):
        return {"tm": place[0], "gy": place[1], "gx": column}

    def is_me(place):
        return jnp.logical_and(place[0] == n, place[1] == g)

    across, block, core = n // (2 * blocks), (n // 2) % blocks, n % 2
    along = ng * block + g
    m = (along + nt - SHIFT) % nt
    t = (2 * across + core + ng) % ng

    s_to = role_of((n + 1) % nt, g)
    s_from = home_of((m + nt - 1) % nt, t)
    fk_along = g + nt - ng // 2 + ng * block + 2 * ((across + chips - g // 2) % chips) + core
    fk_to = role_of((fk_along + nt - SHIFT) % nt, g)
    fk_at = (along - t + ng // 2 + nt) % nt
    fk_from = (2 * blocks * ((t // 2 + (fk_at % ng) // 2) % chips) + 2 * (fk_at // ng) + fk_at % 2, t)
    out_to = home_of(m, t)
    later, earlier = role_of((m + 1) % nt, t), role_of((m + nt - 1) % nt, t)
    near = [(-1, -1), (-1, 1), (1, -1), (1, 1), (-1, 0), (1, 0), (0, -1), (0, 1)]
    wide = near[:6] + [(-2, 0), (2, 0)] + near[6:]

    def neighbour(dx, dy, ahead=0):
        return device(role_of((m + ahead + nt) % nt, (t + dx + ng) % ng), (y + dy + nx) % nx)

    barrier = pltpu.get_barrier_semaphore()
    partners = [device(place, y) for place in (s_from, fk_from, later)]
    partners += [neighbour(dx, dy) for dx, dy in wide] + [neighbour(dx, dy, -1) for dx, dy in [(0, 0)] + near]
    for partner in partners:
        pl.semaphore_signal(barrier, inc=1, device_id=partner, device_id_type=pl.DeviceIdType.MESH)
    pl.semaphore_wait(barrier, len(partners))

    used = [0]
    started = []

    def remote(src, dst, where):
        index = used[0]
        used[0] += 1
        return pltpu.make_async_remote_copy(
            src_ref=src, dst_ref=dst, send_sem=send_sem.at[index], recv_sem=recv_sem.at[index],
            device_id=where, device_id_type=pl.DeviceIdType.MESH), index

    def move(src, dst, place, column, when=None):
        copy, index = remote(src, dst, device(place, column))
        local = pltpu.make_async_copy(src, dst, recv_sem.at[index])
        away = jnp.logical_not(is_me(place))
        if when is not None:
            here = jnp.logical_and(when, is_me(place))
            away = jnp.logical_and(when, away)
        else:
            here = is_me(place)

        @pl.when(away)
        def _():
            copy.start()

        @pl.when(here)
        def _():
            local.start()

        started.append((copy, away))
        return copy

    def piece(dx, dy, own_x, count, width_x, width_y, corner_x, corner_y):
        planes = count if dx == 0 else min(count, width_x - count * (abs(dx) - 1))
        rows_sent = ROWS if dy == 0 else width_y
        if dx != 0 and dy != 0:
            planes, rows_sent = corner_x, corner_y
        from_x = own_x + count - planes if dx > 0 else own_x
        from_y = OWN + ROWS - rows_sent if dy > 0 else OWN
        to_x, to_y = from_x - dx * count, from_y - dy * ROWS
        return (pl.ds(from_x, planes), pl.ds(from_y, rows_sent)), (pl.ds(to_x, planes), pl.ds(to_y, rows_sent))

    def exchange(buf, first, fields, where, *sizes):
        copies = []
        for dx, dy in where:
            src, dst = piece(dx, dy, *sizes)
            copy, _ = remote(buf.at[(pl.ds(first, fields), *src)], buf.at[(pl.ds(first, fields), *dst)], neighbour(dx, dy))
            copy.start()
            started.append((copy, None))
            copies.append(copy)
        return copies

    onward = m < nt - 1

    def hand_on(src, dst, kept, dx=0, dy=0):
        copy, index = remote(src, dst, neighbour(dx, dy, 1))
        stay = pltpu.make_async_copy(kept, dst, recv_sem.at[index])

        @pl.when(onward)
        def _():
            copy.start()

        @pl.when(m == 0)
        def _():
            stay.start()

        started.append((copy, onward))
        return copy

    def arrive(copies):
        for copy in copies:
            copy.wait_recv()

    own = (pl.ds(0, 2), pl.ds(HALO, PLANES), pl.ds(OWN, ROWS))
    s_sizes = (HALO, PLANES, HALO, HALO, 4, 4)

    fk_own = (pl.ds(4, PLANES), pl.ds(OWN, ROWS))
    first_s = s_buf.at[0]
    last_home = n == nt - 1
    s_in = []
    for field in range(2):
        part = (field, *own[1:])
        mark = used[0]
        s_in.append(move(guess_ref.at[0, field], first_s.at[part], s_to, y, jnp.logical_not(last_home)))
        used[0] = mark
        move(init_ref.at[field], first_s.at[part], s_to, y, last_home)
    feed_in = move(feed_ref, fk_buf.at[(0, *fk_own)], fk_to, y)
    kill_in = move(kill_ref, fk_buf.at[(1, *fk_own)], fk_to, y)

    row = lax.broadcasted_iota(jnp.int32, (WINDOW, LANES), 0)
    lane = lax.broadcasted_iota(jnp.int32, (WINDOW, LANES), 1)
    even_row, even_lane = row % 2 == 0, lane % 2 == 0

    def rows(by=0):
        return pl.ds(LOW + by, WINDOW)

    def turn(value, by, axis):
        size = value.shape[axis]
        return pltpu.roll(value, by % size, axis % value.ndim)

    def source(lap_u, lap_v, u, v, feed, both):
        reaction = u * v * v
        return lap_u - reaction + feed * (1.0 - u), lap_v + reaction - both * v

    def fine_rates(buf, first, at, feed_at, count):
        laps, mids = [], []
        for field in range(2):
            f = first + field
            mid = buf[f, pl.ds(at, count), rows(), :]
            total = buf[f, pl.ds(at - 1, count), rows(), :] + buf[f, pl.ds(at + 1, count), rows(), :]
            total = total + buf[f, pl.ds(at, count), rows(-1), :] + buf[f, pl.ds(at, count), rows(1), :]
            total = total + turn(mid, 1, -1) + turn(mid, -1, -1)
            laps.append(DIFF[field] * (total - 6.0 * mid))
            mids.append(mid)
        feed = fk_buf[0, pl.ds(feed_at, count), rows(), :]
        both = fk_buf[2, pl.ds(feed_at, count), rows(), :]
        return mids, source(laps[0], laps[1], mids[0], mids[1], feed, both)

    def pair_sum(value):
        value = value + jnp.where(even_row, turn(value, -1, -2), turn(value, 1, -2))
        return value + jnp.where(even_lane, turn(value, -1, -1), turn(value, 1, -1))

    def restrict(first, second):
        return 0.125 * pair_sum(first + second)

    def coarse_rates(below, mid, above, feed, both):
        laps = []
        for field in range(2):
            total = below[field] + above[field] + turn(mid[field], 2, -2) + turn(mid[field], -2, -2)
            total = total + turn(mid[field], 2, -1) + turn(mid[field], -2, -1)
            laps.append((0.25 * DIFF[field]) * (total - 6.0 * mid[field]))
        return source(laps[0], laps[1], mid[0], mid[1], feed, both)

    def pack(planes):
        mixed = [jnp.where(even_lane, plane[0], plane[1]) for plane in planes]
        return jnp.where(even_row, mixed[0], mixed[1])

    def unpack(packed):
        planes = [jnp.where(even_row, packed, turn(packed, 1, -2)), jnp.where(even_row, turn(packed, -1, -2), packed)]
        return [[jnp.where(even_lane, plane, turn(plane, 1, -1)), jnp.where(even_lane, turn(plane, -1, -1), plane)]
                for plane in planes]

    def send_states(buf, first, fields):
        return exchange(buf, first, fields, wide, *s_sizes)

    s_halo, c_halo, fk_halo = [], [], []
    for field in range(2):
        arrive((s_in[field],))
        s_halo += send_states(first_s, field, 1)
    pl.semaphore_signal(home_sem, inc=1, device_id=device(earlier, y), device_id_type=pl.DeviceIdType.MESH)
    for field, moved in enumerate((feed_in, kill_in)):
        arrive((moved,))
        fk_halo += exchange(fk_buf, field, 1, near, 4, PLANES, 4, 4, 3, 3)
    arrive(fk_halo)
    for p in range(0, 12, 2):
        both = fk_buf[0, pl.ds(p, 2), rows(), :] + fk_buf[1, pl.ds(p, 2), rows(), :]
        fk_buf[2, pl.ds(p, 2), rows(), :] = both
    coarse_feed, coarse_both = [], []
    for p in range(4):
        feed, kill = [restrict(fk_buf[f, 2 + 2 * p, rows(), :], fk_buf[f, 3 + 2 * p, rows(), :]) for f in range(2)]
        coarse_feed.append(feed)
        coarse_both.append(feed + kill)

    for k in range(ITERS):
        s_now, c_now = s_buf.at[k], c_buf.at[k]
        last = k == ITERS - 1
        if k > 0:
            u_old = u_buf.at[k - 1]
            arrive(u_halo)
            for p in range(0, 12, 2):
                _, one = fine_rates(u_old, 0, p + 1, p, 2)
                _, two = fine_rates(u_old, 2, p + 1, p, 2)
                for field in range(2):
                    zero = g0_buf[field, pl.ds(p, 2), rows(), :]
                    a0_buf[field, pl.ds(p, 2), rows(), :] = (
                        (WEIGHTS[0][0] - HALF_STEP) * zero + WEIGHTS[0][1] * one[field] + WEIGHTS[0][2] * two[field])
                    a1_buf[field, pl.ds(p, 2), rows(), :] = (
                        WEIGHTS[1][0] * zero + (WEIGHTS[1][1] - HALF_STEP) * one[field] + WEIGHTS[1][2] * two[field])
        arrive(s_halo)
        for p in range(0, 12, 2):
            mids, rates = fine_rates(s_now, 0, p + 1, p, 2)
            for field in range(2):
                node = mids[field] + HALF_STEP * rates[field]
                if k > 0:
                    node = node + a0_buf[field, pl.ds(p, 2), rows(), :]
                g0_buf[field, pl.ds(p, 2), rows(), :] = rates[field]
                v1_buf[field, pl.ds(p, 2), rows(), :] = node
        for p in range(0, 10, 2):
            mids, rates = fine_rates(v1_buf, 0, p + 1, p + 1, 2)
            for field in range(2):
                node = mids[field] + HALF_STEP * rates[field]
                if k > 0:
                    node = node + a1_buf[field, pl.ds(p + 1, 2), rows(), :]
                v2_buf[field, pl.ds(p, 2), rows(), :] = node
                g1_buf[field, pl.ds(p, 2), rows(), :] = rates[field]
        rest_s = [[restrict(s_now[f, 1 + 2 * p, rows(), :], s_now[f, 2 + 2 * p, rows(), :]) for f in range(2)]
                  for p in range(6)]
        if k == 0:
            coarse = rest_s
            for p in range(3):
                c_now[p, rows(), :] = pack(coarse[2 * p : 2 * p + 2])
        else:
            arrive(c_halo)
            coarse = [plane for p in range(3) for plane in unpack(c_now[p, rows(), :])]
        w_one, late = [], []
        for p in range(4):
            _, two = fine_rates(v2_buf, 0, 2 * p + 1, 2 * p + 2, 2)
            rate_c = coarse_rates(coarse[p], coarse[p + 1], coarse[p + 2], coarse_feed[p], coarse_both[p])
            rate_s = coarse_rates(rest_s[p], rest_s[p + 1], rest_s[p + 2], coarse_feed[p], coarse_both[p])
            values, later_sums = [], []
            for f in range(2):
                zero = g0_buf[f, pl.ds(2 + 2 * p, 2), rows(), :]
                one = g1_buf[f, pl.ds(1 + 2 * p, 2), rows(), :]
                first, second = [w[0] * zero + w[1] * one + w[2] * two[f] for w in WEIGHTS]
                values.append(coarse[p + 1][f] + HALF_STEP * (rate_c[f] - rate_s[f]) + restrict(first[0], first[1]))
                later_sums.append(restrict(second[0], second[1]) if p in (1, 2) else None)
            w_one.append(values)
            late.append(later_sums)
        rest_v1 = [[restrict(v1_buf[f, 2 + 2 * p, rows(), :], v1_buf[f, 3 + 2 * p, rows(), :]) for f in range(2)]
                   for p in range(4)]
        keep = slice(OWN - LOW, OWN - LOW + ROWS)
        w_two = []
        for p in (1, 2):
            w_two.append([])
            rate_w = coarse_rates(w_one[p - 1], w_one[p], w_one[p + 1], coarse_feed[p], coarse_both[p])
            rate_v1 = coarse_rates(rest_v1[p - 1], rest_v1[p], rest_v1[p + 1], coarse_feed[p], coarse_both[p])
            for f in range(2):
                w_end = w_one[p][f] + HALF_STEP * (rate_w[f] - rate_v1[f]) + late[p][f]
                w_two[-1].append(w_end)
                rest_v2 = restrict(v2_buf[f, 1 + 2 * p, rows(), :], v2_buf[f, 2 + 2 * p, rows(), :])
                for at in (2 * p - 2, 2 * p - 1):
                    two = v2_buf[f, 3 + at, rows(), :] + (w_end - rest_v2)
                    if last:
                        o_buf[f, at, :, :] = two[keep]
                    else:
                        one = v1_buf[f, 4 + at, rows(), :] + (w_one[p][f] - rest_v1[p][f])
                        u_buf[k, f, HALO + at, pl.ds(OWN, ROWS), :] = one[keep]
                        u_buf[k, 2 + f, HALO + at, pl.ds(OWN, ROWS), :] = two[keep]
        if not last:
            w_buf[k, :, :] = pack(w_two)[keep]
            u_now, s_next, c_next = u_buf.at[k], s_buf.at[k + 1], c_buf.at[k + 1]
            shifted = [
                hand_on(u_now.at[(2 + f, *own[1:])], s_next.at[(f, *own[1:])], s_now.at[(f, *own[1:])]) for f in range(2)
            ]
            s_halo = []
            for dx, dy in near:
                if dx != 0 and dy != 0:
                    src, dst = piece(dx, dy, *s_sizes)
                    src, dst = (pl.ds(2, 2), *src), (pl.ds(0, 2), *dst)
                    s_halo.append(hand_on(u_now.at[src], s_next.at[dst], s_now.at[dst], dx, dy))
            c_halo = []
            for dx, dy in [(0, 0)] + near:
                sent = ROWS if dy == 0 else 4
                from_y = ROWS - sent if dy > 0 else 0
                src, dst = pl.ds(from_y, sent), (1 - dx, pl.ds(OWN + from_y - dy * ROWS, sent))
                c_halo.append(hand_on(w_buf.at[k, src], c_next.at[dst], c_now.at[dst], dx, dy))
            u_halo = send_states(u_now, 0, 4)
            for field in range(2):
                arrive(shifted[field : field + 1])
                s_halo += exchange(s_next, field, 1, wide[4:], *s_sizes)

    pl.semaphore_wait(home_sem, 1)
    out_in = move(o_buf, out_ref.at[0], out_to, y)
    arrive((out_in,))
    for copy, when in started:
        if when is None:
            copy.wait_send()
        else:

            @pl.when(when)
            def _(copy=copy):
                copy.wait_send()

    assert used[0] <= N_SEMS


def solution(mesh):
    dims = (mesh.shape["tm"], mesh.shape["gy"], mesh.shape["gx"])

    def shards(initial_state, slice_guess, feed_rate, kill_rate):
        buffers = [
            (ITERS, 2, 14, TALL, LANES),
            (ITERS, 3, TALL, LANES),
            (ITERS - 1, 4, 14, TALL, LANES),
            (ITERS - 1, ROWS, LANES),
            (2, 12, TALL, LANES),
            (2, 10, TALL, LANES),
            (3, 12, TALL, LANES),
            (2, 12, TALL, LANES),
            (2, 10, TALL, LANES),
            (2, 12, TALL, LANES),
            (2, 12, TALL, LANES),
            (2, PLANES, ROWS, LANES),
        ]
        return pl.pallas_call(
            functools.partial(kernel, dims),
            out_shape=jax.ShapeDtypeStruct((1, 2, PLANES, ROWS, LANES), jnp.float32),
            in_specs=[pl.BlockSpec(memory_space=pl.ANY)] * 4,
            out_specs=pl.BlockSpec(memory_space=pl.ANY),
            scratch_shapes=[pltpu.VMEM(shape, jnp.float32) for shape in buffers]
            + [pltpu.SemaphoreType.DMA((N_SEMS,)), pltpu.SemaphoreType.DMA((N_SEMS,)), pltpu.SemaphoreType.REGULAR],
            compiler_params=pltpu.CompilerParams(collective_id=0, has_side_effects=True),
        )(initial_state, slice_guess, feed_rate, kill_rate)

    in_specs = (
        P(None, "gy", "gx", None),
        P("tm", None, "gy", "gx", None),
        P("gy", "gx", None),
        P("gy", "gx", None),
    )
    out_specs = P("tm", None, "gy", "gx", None)
    return jax.shard_map(shards, mesh=mesh, in_specs=in_specs, out_specs=out_specs, check_vma=False)
```
